256 devices in a mesh: row: 8 (over y_lo, x), col: 32 (over y_hi, z, core).
Axes of the slice: x: 4, y: 4 (y_hi: 2, y_lo: 2; y = y_hi * 2 + y_lo), z: 8, core: 2. Of those that a mesh axis runs over, the one named last changes fastest.
Arguments:
- volume_plane: bfloat16 [2, 4096, 4096], P(None, 'row', 'col'), may hold values from -4 to 4
- wave_a: bfloat16 [2, 4096, 4096], P(None, 'row', 'col'), may hold values from -4 to 4
- wave_b: bfloat16 [2, 4096, 4096], P(None, 'col', 'row'), may hold values from -4 to 4
- shift_rows: int32 [2, 2, 4096], P(None, None, 'row'), may hold values from -864 to 864, as said below
- fraction_rows: float32 [2, 2, 4096], P(None, None, 'row'), may hold values from -0.5 to 0.5
- shift_columns: int32 [2, 4096], P(None, 'col'), may hold values from -1728 to 1728, as said below
- fraction_columns: float32 [2, 4096], P(None, 'col'), may hold values from -0.5 to 0.5
- travel_distance: float32 [2], replicated, may hold values from 16 to 32
Outputs:
- exit_a: bfloat16 [2, 4096, 4096], P(None, 'row', 'col')
- exit_b: bfloat16 [2, 4096, 4096], P(None, 'col', 'row')
The draws below stay inside these ranges and needn't reach their ends.
Inputs may be any that keep to these rules, and one draw needn't show every extreme that they name: For view v, both shift_rows[v, 0] and shift_rows[v, 1] equal -s_v floor((2 r - 4095) m_v / 4095) for row r, with a sign s_v of 1 or -1 and a whole magnitude m_v from 432 to 864; m_0 = 864. shift_columns[v, c] = s_v floor((2 c - 4095) 2 m_v / 4095) with the s_v and m_v of shift_rows.
All inputs are finite; a program needn't handle non-finite values.
Results may differ from the reference program's by a relative error of at most 0.018.
Values may be sent and summed in bfloat16 or wider, within the bound.
A program may use at most 64 MiB of HBM per device.

```python
import math
import jax
import jax.numpy as jnp
from jax import lax

BLOCK = 128
MARGIN = 32
SHIFT_X = 864
SHIFT_Y = 1728
PLANE = 4096


def shear_sizes(key):
    base = jax.random.fold_in(key, 4242)
    magnitudes = jax.random.randint(jax.random.fold_in(base, 1), (2,), SHIFT_X // 2, SHIFT_X + 1)
    magnitudes = jnp.where(jnp.arange(2) == 0, SHIFT_X, magnitudes).astype(jnp.int32)
    signs = (2 * jax.random.randint(jax.random.fold_in(base, 2), (2,), 0, 2) - 1).astype(jnp.int32)
    return (magnitudes, signs)


def linear_profile(magnitude, sign):
    position = jnp.arange(PLANE, dtype=jnp.int32)
    return sign * ((2 * position + 1 - PLANE) * magnitude // (PLANE - 1))


def draw_shift_rows(key, part):
    magnitudes, signs = shear_sizes(key)
    profiles = jnp.stack([linear_profile(magnitudes[member], -signs[member]) for member in range(2)])
    return jnp.stack([profiles, profiles], 1).astype(jnp.int32)


def draw_shift_columns(key, part):
    magnitudes, signs = shear_sizes(key)
    profiles = jnp.stack([linear_profile(2 * magnitudes[member], signs[member]) for member in range(2)])
    return profiles.astype(jnp.int32)


def block_levels(stream_key, shape, split, least, high):
    gain, own = 1.0, jax.random.fold_in(stream_key, 6)
    for dim, blocks in split:
        heights = jnp.exp(jax.random.uniform(jax.random.fold_in(own, dim), (blocks,), jnp.float32, least / len(split), high / len(split)))
        gain = gain * jnp.repeat(heights, shape[dim] // blocks).reshape([-1 if axis == dim else 1 for axis in range(len(shape))])
    return gain


def normal_values(stream_key, dims, spread, limit, pieces=(), held_as=jnp.bfloat16):
    values = jax.random.normal(stream_key, dims, jnp.float32) * spread
    if len(pieces) > 0:
        values = block_levels(stream_key, dims, pieces, -0.22, 0.18) * values
    return jnp.clip(values, min=-limit, max=limit).astype(held_as)


def setup_inputs(seed: int = 0) -> dict:
    seeds = jax.random.split(jax.random.key(seed), 9)
    volume_plane = normal_values(seeds[0], (2, PLANE, PLANE), 1.0, 4.0, ((1, 8), (2, 32)))
    wave_a = normal_values(seeds[1], (2, PLANE, PLANE), 0.7, 4.0, ((1, 8), (2, 32)))
    wave_b = normal_values(seeds[2], (2, PLANE, PLANE), 0.7, 4.0, ((1, 32), (2, 8)))
    shift_rows = draw_shift_rows(jax.random.fold_in(seeds[8], 71), 0)
    fraction_rows = jnp.clip(jax.random.uniform(seeds[4], (2, 2, PLANE), jnp.float32, -0.5, 0.5) * block_levels(seeds[4], (2, 2, PLANE), ((2, 8),), -0.4, 0.0), -0.5, 0.5)
    shift_columns = draw_shift_columns(jax.random.fold_in(seeds[8], 71), 0)
    fraction_columns = jnp.clip(jax.random.uniform(seeds[6], (2, PLANE), jnp.float32, -0.5, 0.5) * block_levels(seeds[6], (2, PLANE), ((1, 32),), -0.4, 0.0), -0.5, 0.5)
    travel_distance = jnp.clip(jax.random.uniform(seeds[7], (2,), jnp.float32, 16.0, 32.0), 16.0, 32.0)
    return dict(volume_plane=volume_plane, wave_a=wave_a, wave_b=wave_b, shift_rows=shift_rows, fraction_rows=fraction_rows, shift_columns=shift_columns, fraction_columns=fraction_columns, travel_distance=travel_distance)


ABSORB = 0.25


def fourier_tables(block_len, margin):
    window_len = block_len + 2 * margin
    frequency = jnp.arange(window_len, dtype=jnp.int32) - window_len // 2
    position = jnp.arange(window_len, dtype=jnp.int32)
    angles = 2.0 * jnp.pi * jnp.mod(position[:, None] * frequency[None, :], window_len).astype(jnp.float32) / window_len
    cosine = jnp.cos(angles)
    sines = jnp.sin(angles)
    forward = jnp.concatenate([jnp.concatenate([cosine, -sines], 1), jnp.concatenate([sines, cosine], 1)], 0).astype(jnp.bfloat16)
    target = jnp.arange(block_len, dtype=jnp.int32) + margin
    inverse_angle = 2.0 * jnp.pi * jnp.mod(frequency[:, None] * target[None, :], window_len).astype(jnp.float32) / window_len
    inverse_cosine = jnp.cos(inverse_angle) / window_len
    inverse_sine = jnp.sin(inverse_angle) / window_len
    inverse = jnp.concatenate([jnp.concatenate([inverse_cosine, inverse_sine], 1), jnp.concatenate([-inverse_sine, inverse_cosine], 1)], 0).astype(jnp.bfloat16)
    return forward, inverse, frequency.astype(jnp.float32)


def shear_ramp(fractions, frequency):
    window_len = frequency.shape[0]
    phases = (-2.0 * jnp.pi / window_len) * fractions[:, None] * frequency[None, :]
    nyquist = (jnp.arange(window_len) == 0)[None, :]
    ramp_real = jnp.where(nyquist, jnp.cos(jnp.pi * fractions)[:, None], jnp.cos(phases))
    ramp_imaginary = jnp.where(nyquist, 0.0, jnp.sin(phases))
    return ramp_real, ramp_imaginary


def travel_ramp(distance, frequency):
    window_len = frequency.shape[0]
    phases = (-2.0 * jnp.pi / (window_len * window_len)) * distance * frequency * frequency
    return jnp.cos(phases)[None, :], jnp.sin(phases)[None, :]


def line_pass(padded, extent, shifts, ramp_real, ramp_imaginary, tables):
    forward, inverse = tables[0], tables[1]
    window_len = BLOCK + 2 * MARGIN
    line_count = padded.shape[1]
    blocks = (padded.shape[2] - 2 * extent) // BLOCK
    reach_len = blocks * BLOCK + 2 * MARGIN
    starts = (extent - MARGIN - shifts).astype(jnp.int32)

    def pick(single, start):
        return lax.dynamic_slice_in_dim(single, start, reach_len, 1)

    shifted = jax.vmap(pick, in_axes=(1, 0), out_axes=1)(padded, starts)
    middle = shifted[:, :, MARGIN:MARGIN + blocks * BLOCK].reshape(2, line_count, blocks, BLOCK)
    left_rim = shifted[:, :, :blocks * BLOCK].reshape(2, line_count, blocks, BLOCK)[..., :MARGIN]
    right_rim = shifted[:, :, 2 * MARGIN:2 * MARGIN + blocks * BLOCK].reshape(2, line_count, blocks, BLOCK)[..., BLOCK - MARGIN:]
    windows = jnp.concatenate([left_rim, middle, right_rim], 3)
    spectrum = jnp.einsum("cpms,cst->pmt", windows.astype(jnp.float32), forward.astype(jnp.float32).reshape(2, window_len, 2 * window_len), precision=lax.Precision.HIGHEST)
    spec_real = spectrum[..., :window_len]
    spec_imaginary = spectrum[..., window_len:]
    factor_real = ramp_real[:, None, :]
    factor_imaginary = ramp_imaginary[:, None, :]
    ramped = jnp.concatenate([spec_real * factor_real - spec_imaginary * factor_imaginary, spec_real * factor_imaginary + spec_imaginary * factor_real], -1).astype(jnp.bfloat16)
    result = jnp.einsum("pms,scb->cpmb", ramped.astype(jnp.float32), inverse.astype(jnp.float32).reshape(2 * window_len, 2, BLOCK), precision=lax.Precision.HIGHEST)
    return result.reshape(2, line_count, blocks * BLOCK).astype(jnp.bfloat16)


def blockwise(padded, extent, shifts, ramp_real, ramp_imaginary, tables):
    line_count = padded.shape[1]
    groups = math.gcd(line_count, 512)
    group_count = line_count // groups
    window_len = ramp_real.shape[-1]
    grouped = padded.reshape(2, group_count, groups, padded.shape[2]).transpose(1, 0, 2, 3)
    group_shifts = shifts.reshape(group_count, groups)
    group_real = jnp.broadcast_to(ramp_real, (line_count, window_len)).reshape(group_count, groups, window_len)
    group_imaginary = jnp.broadcast_to(ramp_imaginary, (line_count, window_len)).reshape(group_count, groups, window_len)

    def run_block(payload):
        return line_pass(payload[0], extent, payload[1], payload[2], payload[3], tables)

    finished = lax.map(run_block, (grouped, group_shifts, group_real, group_imaginary))
    return finished.transpose(1, 0, 2, 3).reshape(2, line_count, -1)


def shift_last(plane_data, halo_depth, shifts, fractions, tables):
    padded = jnp.pad(plane_data, ((0, 0), (0, 0), (halo_depth, halo_depth)))
    ramp_real, ramp_imaginary = shear_ramp(fractions, tables[2])
    return blockwise(padded, halo_depth, shifts, ramp_real, ramp_imaginary, tables)


def shift_first(plane_data, halo_depth, shifts, fractions, tables):
    return jnp.swapaxes(shift_last(jnp.swapaxes(plane_data, 1, 2), halo_depth, shifts, fractions, tables), 1, 2)


def travel(wave, distance, tables):
    ramp_real, ramp_imaginary = travel_ramp(distance, tables[2])
    no_shift = jnp.zeros((wave.shape[1],), jnp.int32)
    halfway = blockwise(jnp.pad(wave, ((0, 0), (0, 0), (MARGIN, MARGIN))), MARGIN, no_shift, ramp_real, ramp_imaginary, tables)
    flipped = jnp.swapaxes(halfway, 1, 2)
    no_shift_two = jnp.zeros((flipped.shape[1],), jnp.int32)
    finished = blockwise(jnp.pad(flipped, ((0, 0), (0, 0), (MARGIN, MARGIN))), MARGIN, no_shift_two, ramp_real, ramp_imaginary, tables)
    return jnp.swapaxes(finished, 1, 2)


def transmit(rotated, wave):
    phase_part = rotated[0].astype(jnp.float32)
    absorb_part = rotated[1].astype(jnp.float32)
    amplitude = jnp.exp(-ABSORB * absorb_part)
    through_real = amplitude * jnp.cos(phase_part)
    through_imaginary = amplitude * jnp.sin(phase_part)
    wave_real = wave[0].astype(jnp.float32)
    wave_imaginary = wave[1].astype(jnp.float32)
    return jnp.stack([wave_real * through_real - wave_imaginary * through_imaginary, wave_real * through_imaginary + wave_imaginary * through_real]).astype(jnp.bfloat16)


def reference(volume_plane, wave_a, wave_b, shift_rows, fraction_rows, shift_columns, fraction_columns, travel_distance):
    tables = fourier_tables(BLOCK, MARGIN)
    results = []
    for member in range(2):
        section = shift_last(volume_plane, SHIFT_X + MARGIN, shift_rows[member, 0], fraction_rows[member, 0], tables)
        section = shift_first(section, SHIFT_Y + MARGIN, shift_columns[member], fraction_columns[member], tables)
        section = shift_last(section, SHIFT_X + MARGIN, shift_rows[member, 1], fraction_rows[member, 1], tables)
        results.append(section)
    turned = jnp.swapaxes(jnp.flip(results[1], 2), 1, 2)
    exit_a = travel(transmit(results[0], wave_a), travel_distance[0], tables)
    exit_b = travel(transmit(turned, wave_b), travel_distance[1], tables)
    return exit_a, exit_b
```

```python
import functools

import jax
import jax.numpy as jnp
import numpy as np
from jax import lax
from jax.experimental import pallas as pl
from jax.experimental.pallas import tpu as pltpu
from jax.sharding import PartitionSpec as P

BLOCK = 128
MARGIN = 32
WIN = BLOCK + 2 * MARGIN
HALF = WIN // 2
LINES = 16
ABSORB = 0.25
MESH = pl.DeviceIdType.MESH
BF = jnp.bfloat16
F32 = jnp.float32


def real_tables():
    q = np.arange(HALF + 1)
    p = np.arange(WIN)
    angle = (2.0 * np.pi * np.mod(p[:, None] * q[None, :], WIN).astype(np.float32) / WIN).astype(np.float32)
    forward = np.zeros((WIN, 256), np.float32)
    forward[:, : HALF + 1] = np.cos(angle)
    forward[:, 129 : 128 + HALF] = np.sin(angle)[:, 1:HALF]
    target = np.arange(BLOCK) + MARGIN
    angle = (2.0 * np.pi * np.mod(q[:, None] * target[None, :], WIN).astype(np.float32) / WIN).astype(np.float32)
    weight = np.where((q == 0) | (q == HALF), 1.0, 2.0)[:, None].astype(np.float32)
    inverse = np.zeros((256, BLOCK), np.float32)
    inverse[: HALF + 1] = weight * (np.cos(angle) / WIN)
    inverse[129 : 128 + HALF] = (2.0 * np.sin(angle) / WIN)[1:HALF]
    return forward, inverse


def iota(shape, dim):
    return lax.broadcasted_iota(jnp.int32, shape, dim)


def one_hot(mask):
    return jnp.where(mask, 1.0, 0.0).astype(BF)


def dot(a, b):
    return jnp.dot(a, b, preferred_element_type=F32)


def dot_nt(a, b):
    return lax.dot_general(a, b, (((1,), (1,)), ((), ())), preferred_element_type=F32)


def travel_phase(z, q):
    q = q.astype(F32)
    return (-2.0 * np.pi / (WIN * WIN)) * z * q * q


def kernel(
    nr, nc, vol, wa, wb, srs, scs, trav, sr, fr, sc, fc, fwd, inv, fwdt, invt,
    out_a, out_b,
    wbt, rows0, wrow_a, wrow_b, zone, o1, tile1, turn1, cols, o2, turn2, tile2, rows2, rot, ub, half, ext, extt,
    ramps, tabs, send, recv,
):
    r = lax.axis_index("row")
    c = lax.axis_index("col")
    tile_rows = nc * LINES
    quarters = tile_rows // BLOCK
    col_tiles = nc
    row_tiles = nr * quarters

    barrier = pltpu.get_barrier_semaphore()

    def greet_col(i, _):
        pl.semaphore_signal(barrier, inc=1, device_id={"col": lax.rem(c + i, nc)}, device_id_type=MESH)
        return 0

    def greet_row(i, _):
        pl.semaphore_signal(barrier, inc=1, device_id={"row": lax.rem(r + i, nr)}, device_id_type=MESH)
        return 0

    lax.fori_loop(1, nc, greet_col, 0)
    lax.fori_loop(1, nr, greet_row, 0)
    pl.semaphore_wait(barrier, nc + nr - 2)

    def sixteen(i):
        return pl.ds(pl.multiple_of(i * LINES, LINES), LINES)

    def to_col(phase, src, dst):
        def body(i, _):
            peer = lax.rem(c + i, nc)
            pltpu.make_async_remote_copy(
                src_ref=src(peer), dst_ref=dst, send_sem=send.at[phase], recv_sem=recv.at[phase],
                device_id={"col": peer}, device_id_type=MESH,
            ).start()
            return 0

        lax.fori_loop(1, nc, body, 0)

    def to_row(phase, src, dst):
        def body(i, _):
            peer = lax.rem(r + i, nr)
            pltpu.make_async_remote_copy(
                src_ref=src(peer), dst_ref=dst, send_sem=send.at[phase], recv_sem=recv.at[phase],
                device_id={"row": peer}, device_id_type=MESH,
            ).start()
            return 0

        lax.fori_loop(1, nr, body, 0)

    def arrived(phase, part):
        pltpu.make_async_copy(part, part, recv.at[phase]).wait()

    def left(phase, part):
        pltpu.make_async_copy(part, part, send.at[phase]).wait()

    to_col(0, lambda peer: vol.at[:, sixteen(peer), :], rows0.at[c])
    rows0[c] = vol[:, sixteen(c), :]

    eye = one_hot(iota((BLOCK, BLOCK), 0) == iota((BLOCK, BLOCK), 1))
    anti = one_hot(iota((BLOCK, BLOCK), 0) == BLOCK - 1 - iota((BLOCK, BLOCK), 1))

    lane = iota((LINES, 128), 1)

    def prepare(index, shifts, fractions, start, base, width):
        mine = iota((LINES, width), 1) == start + iota((LINES, width), 0)
        f = jnp.sum(jnp.where(mine, fractions, 0.0), axis=1, keepdims=True)
        k = jnp.sum(jnp.where(mine, shifts.astype(F32), 0.0), axis=1, keepdims=True)
        phase = (2.0 * np.pi / WIN) * f * lane.astype(F32)
        ramps[index, 0] = jnp.cos(phase)
        ramps[index, 1] = jnp.sin(phase)
        ramps[index, 2] = jnp.broadcast_to(k - base.astype(F32), (LINES, 128))
        offset = (-MARGIN - base) & 127
        pick = one_hot(iota((384, WIN), 0) - offset == iota((384, WIN), 1))
        tabs[index] = dot(pick, fwd[...]).astype(BF)

    def row_base(v, p):
        return jnp.minimum(srs[v, p, c * LINES], srs[v, p, c * LINES + LINES - 1])

    def col_base(v):
        return jnp.minimum(scs[v, r * LINES], scs[v, r * LINES + LINES - 1])

    for v in range(2):
        for p in range(2):
            prepare(3 * v + 2 * p, sr[v, pl.ds(p, 1), :], fr[v, pl.ds(p, 1), :], c * LINES, row_base(v, p), tile_rows)
        prepare(3 * v + 1, sc[pl.ds(v, 1), :], fc[pl.ds(v, 1), :], r * LINES, col_base(v), BLOCK)
    tabs[6] = dot(one_hot(iota((384, WIN), 0) - 96 == iota((384, WIN), 1)), fwd[...]).astype(BF)

    for part in range(2):
        flipped = dot(anti, wb[part]).astype(BF)
        for n in range(quarters):
            wbt[part, n * BLOCK : (n + 1) * BLOCK, :] = dot_nt(eye, flipped[:, n * BLOCK : (n + 1) * BLOCK]).astype(BF)

    zone[...] = jnp.zeros(zone.shape, BF)
    for v in range(2):
        ub[v, 0] = jnp.zeros((2, LINES, 128), BF)
        ub[v, col_tiles + 1] = jnp.zeros((2, LINES, 128), BF)

    pad = 14

    def shear(index, base, bits, src, count, dst):
        shift = ramps[index, 2].astype(jnp.int32)
        a = src[...].astype(F32)
        zero = jnp.zeros((1, 2, LINES, 128), F32)
        a = jnp.concatenate([a, zero], 0)
        for bit in range(bits):
            step = 2**bit
            turned = pltpu.roll(a, step, 3)
            before = jnp.concatenate([zero, turned[:-1]], 0)
            moved = jnp.where(lane >= step, turned, before)
            a = jnp.where((shift & step) != 0, moved, a)
        zone[pad : pad + count + 1] = a.astype(BF)
        first = lax.shift_right_arithmetic(-MARGIN - base, 7) + pad
        group = min(16, count)
        cosine = ramps[index, 0]
        sine = ramps[index, 1]

        def chunk(g, _):
            m = g * group
            pieces = [zone[pl.ds(first + m + i, group)].reshape(group * 2 * LINES, 128) for i in range(3)]
            spectrum = dot(jnp.concatenate(pieces, 1), tabs[index])
            even = spectrum[:, :128].reshape(group * 2, LINES, 128)
            odd = spectrum[:, 128:].reshape(group * 2, LINES, 128)
            y = jnp.concatenate([even * cosine - odd * sine, odd * cosine + even * sine], 2)
            line = dot(y.reshape(group * 2 * LINES, 256).astype(BF), inv[...])
            dst[pl.ds(m, group)] = line.reshape(group, 2, LINES, 128).astype(BF)
            return 0

        lax.fori_loop(0, count // group, chunk, 0)

    for v in range(2):
        if v == 0:
            arrived(0, rows0.at[pl.ds(0, nc - 1)])
        shear(3 * v, row_base(v, 0), 3, rows0, col_tiles, o1.at[v])
        to_col(3 + v, lambda peer, v=v: o1.at[v, peer], tile1.at[v, :, sixteen(c), :])
        tile1[v, :, sixteen(c), :] = o1[v, c]

    to_col(1, lambda peer: wa.at[:, sixteen(peer), :], wrow_a.at[c])
    wrow_a[c] = wa[:, sixteen(c), :]
    to_col(2, lambda peer: wbt.at[:, sixteen(peer), :], wrow_b.at[nc - 1 - c])
    wrow_b[nc - 1 - c] = wbt[:, sixteen(c), :]

    for v in range(2):
        arrived(3 + v, tile1.at[v, :, pl.ds(0, tile_rows - LINES), :])
        for part in range(2):
            t = dot_nt(eye, tile1[v, part]).astype(BF)
            for n in range(quarters):
                turn1[v, n, part] = t[:, n * BLOCK : (n + 1) * BLOCK]
        to_row(
            5 + v,
            lambda peer, v=v: turn1.at[v, :, :, sixteen(peer), :],
            cols.at[v, pl.ds(r * quarters, quarters)],
        )
        cols[v, pl.ds(r * quarters, quarters)] = turn1[v, :, :, sixteen(r), :]

    for v in range(2):
        arrived(5 + v, cols.at[v, pl.ds(0, row_tiles - quarters)])
        shear(3 * v + 1, col_base(v), 4, cols.at[v], row_tiles, o2.at[v])
        to_row(
            7 + v,
            lambda peer, v=v: o2.at[v, pl.ds(peer * quarters, quarters)],
            turn2.at[v, :, :, sixteen(r), :],
        )
        turn2[v, :, :, sixteen(r), :] = o2[v, pl.ds(r * quarters, quarters)]

    for v in range(2):
        arrived(7 + v, turn2.at[v, :, :, pl.ds(0, BLOCK - LINES), :])
        for part in range(2):
            for n in range(quarters):
                tile2[v, part, n * BLOCK : (n + 1) * BLOCK, :] = dot_nt(eye, turn2[v, n, part]).astype(BF)
        to_col(9 + v, lambda peer, v=v: tile2.at[v, :, sixteen(peer), :], rows2.at[v, c])
        rows2[v, c] = tile2[v, :, sixteen(c), :]

    for v in range(2):
        wave = (wrow_a, wrow_b)[v]
        arrived(9 + v, rows2.at[v, pl.ds(0, nc - 1)])
        shear(3 * v + 2, row_base(v, 1), 3, rows2.at[v], col_tiles, rot)
        arrived(1 + v, wave.at[pl.ds(0, nc - 1)])
        group = 4

        def through(g, _, v=v, wave=wave):
            m = g * group
            block = rot[pl.ds(m, group)].astype(F32)
            w = wave[pl.ds(m, group)].astype(F32)
            amplitude = jnp.exp(-ABSORB * block[:, 1])
            real = amplitude * jnp.cos(block[:, 0])
            imaginary = amplitude * jnp.sin(block[:, 0])
            ub[v, pl.ds(1 + m, group), 0] = (w[:, 0] * real - w[:, 1] * imaginary).astype(BF)
            ub[v, pl.ds(1 + m, group), 1] = (w[:, 0] * imaginary + w[:, 1] * real).astype(BF)
            return 0

        lax.fori_loop(0, col_tiles // group, through, 0)
        phase = travel_phase(trav[v], iota((1, 256), 1) & 127)
        factor_real = jnp.cos(phase)
        factor_imaginary = jnp.sin(phase)
        span = min(16, col_tiles)

        def travel(g, _, v=v, factor_real=factor_real, factor_imaginary=factor_imaginary):
            m = g * span
            pieces = [ub[v, pl.ds(m + i, span)].reshape(span * 2 * LINES, 128) for i in range(3)]
            spectrum = dot(jnp.concatenate(pieces, 1), tabs[6]).reshape(span, 2, LINES, 256)
            a, b = spectrum[:, 0], spectrum[:, 1]
            y = jnp.stack([factor_real * a - factor_imaginary * b, factor_real * b + factor_imaginary * a], 1)
            line = dot(y.reshape(span * 2 * LINES, 256).astype(BF), inv[...])
            half[v, pl.ds(m, span)] = line.reshape(span, 2, LINES, 128).astype(BF)
            return 0

        lax.fori_loop(0, col_tiles // span, travel, 0)
        spot = pl.ds(pl.multiple_of(MARGIN + c * LINES, LINES), LINES)
        if v == 0:
            to_col(11, lambda peer: half.at[0, peer], ext.at[0, :, spot, :])
            ext[0, :, spot, :] = half[0, c]
        else:
            to_col(12, lambda peer: half.at[1, nc - 1 - peer], ext.at[1, :, spot, :])
            ext[1, :, spot, :] = half[1, nc - 1 - c]

    top = pl.ds(0, MARGIN)
    bottom = pl.ds(MARGIN + tile_rows, MARGIN)
    head = pl.ds(MARGIN, MARGIN)
    tail = pl.ds(tile_rows, MARGIN)

    def down(v):
        return pltpu.make_async_remote_copy(
            src_ref=ext.at[v, :, tail, :], dst_ref=ext.at[v, :, top, :], send_sem=send.at[13 + v],
            recv_sem=recv.at[13 + v], device_id={"row": lax.rem(r + 1, nr)}, device_id_type=MESH,
        )

    def up(v):
        return pltpu.make_async_remote_copy(
            src_ref=ext.at[v, :, head, :], dst_ref=ext.at[v, :, bottom, :], send_sem=send.at[15 + v],
            recv_sem=recv.at[15 + v], device_id={"row": lax.rem(r + nr - 1, nr)}, device_id_type=MESH,
        )

    for v in range(2):
        arrived(11 + v, ext.at[v, :, pl.ds(0, tile_rows - LINES), :])

        @pl.when(r < nr - 1)
        def _(v=v):
            down(v).start()

        @pl.when(r > 0)
        def _(v=v):
            up(v).start()

        @pl.when(r == 0)
        def _(v=v):
            ext[v, :, top, :] = jnp.zeros((2, MARGIN, 128), BF)

        @pl.when(r == nr - 1)
        def _(v=v):
            ext[v, :, bottom, :] = jnp.zeros((2, MARGIN, 128), BF)

    for v in range(2):

        @pl.when(r > 0)
        def _(v=v):
            down(v).wait_recv()

        @pl.when(r < nr - 1)
        def _(v=v):
            up(v).wait_recv()

        if v == 0:
            phase = travel_phase(trav[0], iota((256, 128), 0) & 127)
            factor_real = jnp.cos(phase)
            factor_imaginary = jnp.sin(phase)
            for n in range(quarters):
                window = jnp.concatenate([ext[0, part, n * BLOCK : n * BLOCK + WIN, :] for part in range(2)], 1)
                spectrum = dot(fwdt[...], window)
                a, b = spectrum[:, :128], spectrum[:, 128:]
                y = jnp.concatenate(
                    [factor_real * a - factor_imaginary * b, factor_real * b + factor_imaginary * a], 1
                ).astype(BF)
                line = dot(invt[...], y).astype(BF)
                out_a[0, n * BLOCK : (n + 1) * BLOCK, :] = line[:, :128]
                out_a[1, n * BLOCK : (n + 1) * BLOCK, :] = line[:, 128:]
        else:
            phase = travel_phase(trav[1], iota((1, 256), 1) & 127)
            factor_real = jnp.cos(phase)
            factor_imaginary = jnp.sin(phase)
            for part in range(2):
                extt[part, :, 0 : tile_rows + 2 * MARGIN] = dot_nt(anti, ext[1, part]).astype(BF)
                extt[part, :, tile_rows + 2 * MARGIN :] = jnp.zeros((BLOCK, MARGIN * 2), BF)
            for n in range(quarters):
                window = extt[:, :, n * BLOCK : (n + 2) * BLOCK].reshape(2 * BLOCK, 2 * BLOCK)
                spectrum = dot(window[:, :WIN], fwd[...])
                a, b = spectrum[:BLOCK], spectrum[BLOCK:]
                y = jnp.concatenate(
                    [factor_real * a - factor_imaginary * b, factor_real * b + factor_imaginary * a], 0
                ).astype(BF)
                line = dot(y, inv[...]).astype(BF)
                out_b[0, :, n * BLOCK : (n + 1) * BLOCK] = line[:BLOCK]
                out_b[1, :, n * BLOCK : (n + 1) * BLOCK] = line[BLOCK:]

    left(0, vol.at[:, pl.ds(0, tile_rows - LINES), :])
    left(1, wa.at[:, pl.ds(0, tile_rows - LINES), :])
    left(2, wbt.at[:, pl.ds(0, tile_rows - LINES), :])
    for v in range(2):
        left(3 + v, o1.at[v, pl.ds(0, nc - 1)])
        left(5 + v, turn1.at[v, :, :, pl.ds(0, BLOCK - LINES), :])
        left(7 + v, o2.at[v, pl.ds(0, row_tiles - quarters)])
        left(9 + v, tile2.at[v, :, pl.ds(0, tile_rows - LINES), :])
        left(11 + v, half.at[v, pl.ds(0, nc - 1)])

        @pl.when(r < nr - 1)
        def _(v=v):
            down(v).wait_send()

        @pl.when(r > 0)
        def _(v=v):
            up(v).wait_send()


def on_device(nr, nc, vol, wa, wb, sr, fr, sc, fc, trav):
    forward, inverse = real_tables()
    tile_rows = nc * LINES
    quarters = tile_rows // BLOCK
    col_tiles, row_tiles = nc, nr * quarters
    vmem = pl.BlockSpec(memory_space=pltpu.VMEM)
    smem = pl.BlockSpec(memory_space=pltpu.SMEM)
    lines = (2, LINES, 128)
    scratch = [
        pltpu.VMEM((2, tile_rows, 128), BF),
        pltpu.VMEM((col_tiles, *lines), BF),
        pltpu.VMEM((col_tiles, *lines), BF),
        pltpu.VMEM((col_tiles, *lines), BF),
        pltpu.VMEM((64, *lines), BF),
        pltpu.VMEM((2, col_tiles, *lines), BF),
        pltpu.VMEM((2, 2, tile_rows, 128), BF),
        pltpu.VMEM((2, quarters, 2, BLOCK, 128), BF),
        pltpu.VMEM((2, row_tiles, *lines), BF),
        pltpu.VMEM((2, row_tiles, *lines), BF),
        pltpu.VMEM((2, quarters, 2, BLOCK, 128), BF),
        pltpu.VMEM((2, 2, tile_rows, 128), BF),
        pltpu.VMEM((2, col_tiles, *lines), BF),
        pltpu.VMEM((col_tiles, *lines), BF),
        pltpu.VMEM((2, col_tiles + 2, *lines), BF),
        pltpu.VMEM((2, col_tiles, *lines), BF),
        pltpu.VMEM((2, 2, tile_rows + 2 * MARGIN, 128), BF),
        pltpu.VMEM((2, BLOCK, tile_rows + BLOCK), BF),
        pltpu.VMEM((6, 3, LINES, 128), F32),
        pltpu.VMEM((7, 384, 256), BF),
        pltpu.SemaphoreType.DMA((17,)),
        pltpu.SemaphoreType.DMA((17,)),
    ]
    return pl.pallas_call(
        functools.partial(kernel, nr, nc),
        out_shape=(
            jax.ShapeDtypeStruct((2, tile_rows, 128), BF),
            jax.ShapeDtypeStruct((2, 128, tile_rows), BF),
        ),
        in_specs=[vmem] * 3 + [smem] * 3 + [vmem] * 8,
        out_specs=(vmem, vmem),
        scratch_shapes=scratch,
        compiler_params=pltpu.CompilerParams(
            collective_id=0, has_side_effects=True, vmem_limit_bytes=56 * 2**20
        ),
        name="rotate_travel",
    )(
        vol, wa, wb, sr, sc, trav, sr, fr, sc, fc,
        jnp.asarray(forward, BF), jnp.asarray(inverse, BF),
        jnp.asarray(forward.T, BF), jnp.asarray(inverse.T, BF),
    )


def solution(mesh):
    nr, nc = mesh.shape["row"], mesh.shape["col"]
    return jax.shard_map(
        functools.partial(on_device, nr, nc),
        mesh=mesh,
        in_specs=(
            P(None, "row", "col"),
            P(None, "row", "col"),
            P(None, "col", "row"),
            P(None, None, "row"),
            P(None, None, "row"),
            P(None, "col"),
            P(None, "col"),
            P(),
        ),
        out_specs=(P(None, "row", "col"), P(None, "col", "row")),
        check_vma=False,
    )
```

```python
import functools

import jax
import jax.numpy as jnp
import numpy as np
from jax import lax
from jax.experimental import pallas as pl
from jax.experimental.pallas import tpu as pltpu
from jax.sharding import PartitionSpec as P

BLOCK = 128
MARGIN = 32
WIN = BLOCK + 2 * MARGIN
HALF = WIN // 2
LINES = 16
ABSORB = 0.25
MESH = pl.DeviceIdType.MESH
BF = jnp.bfloat16
F32 = jnp.float32


def real_tables():
    q = np.arange(HALF + 1)
    p = np.arange(WIN)
    angle = (2.0 * np.pi * np.mod(p[:, None] * q[None, :], WIN).astype(np.float32) / WIN).astype(np.float32)
    forward = np.zeros((WIN, 256), np.float32)
    forward[:, : HALF + 1] = np.cos(angle)
    forward[:, 129 : 128 + HALF] = np.sin(angle)[:, 1:HALF]
    target = np.arange(BLOCK) + MARGIN
    angle = (2.0 * np.pi * np.mod(q[:, None] * target[None, :], WIN).astype(np.float32) / WIN).astype(np.float32)
    weight = np.where((q == 0) | (q == HALF), 1.0, 2.0)[:, None].astype(np.float32)
    inverse = np.zeros((256, BLOCK), np.float32)
    inverse[: HALF + 1] = weight * (np.cos(angle) / WIN)
    inverse[129 : 128 + HALF] = (2.0 * np.sin(angle) / WIN)[1:HALF]
    return forward, inverse


def iota(shape, dim):
    return lax.broadcasted_iota(jnp.int32, shape, dim)


def one_hot(mask):
    return jnp.where(mask, 1.0, 0.0).astype(BF)


def dot(a, b):
    return jnp.dot(a, b, preferred_element_type=F32)


def dot_nt(a, b):
    return lax.dot_general(a, b, (((1,), (1,)), ((), ())), preferred_element_type=F32)


def travel_phase(z, q):
    q = q.astype(F32)
    return (-2.0 * np.pi / (WIN * WIN)) * z * q * q


def kernel(
    nr, nc, vol, wa, wb, srs, scs, trav, sr, fr, sc, fc, fwd, inv, fwdt, invt,
    out_a, out_b,
    wbt, rows0, wrow_a, wrow_b, zone, o1, tile1, turn1, cols, o2, turn2, tile2, rows2, rot, ub, half, ext, extt,
    ramps, tabs, send, recv,
):
    r = lax.axis_index("row")
    c = lax.axis_index("col")
    tile_rows = nc * LINES
    quarters = tile_rows // BLOCK
    col_tiles = nc
    row_tiles = nr * quarters

    barrier = pltpu.get_barrier_semaphore()

    def greet_col(i, _):
        pl.semaphore_signal(barrier, inc=1, device_id={"col": lax.rem(c + i, nc)}, device_id_type=MESH)
        return 0

    def greet_row(i, _):
        pl.semaphore_signal(barrier, inc=1, device_id={"row": lax.rem(r + i, nr)}, device_id_type=MESH)
        return 0

    lax.fori_loop(1, nc, greet_col, 0)
    lax.fori_loop(1, nr, greet_row, 0)
    pl.semaphore_wait(barrier, nc + nr - 2)

    def sixteen(i):
        return pl.ds(pl.multiple_of(i * LINES, LINES), LINES)

    depth = nc // 4
    width = nr // 2
    zone_z, core = lax.rem(lax.div(c, 2), depth), lax.rem(c, 2)
    side_c, side_r = lax.div(c, 2 * depth), lax.div(r, width)
    place = lax.rem(r, width)

    def hop(position, ring):
        step = lax.div(position + 1, 2)
        return jnp.where(lax.rem(position, 2) == 1, ring // 2 - step, ring // 2 + step)

    def ship(src, dst, phase, landing, axis, peer):
        pltpu.make_async_remote_copy(
            src_ref=src(peer), dst_ref=dst, send_sem=send.at[phase], recv_sem=recv.at[landing],
            device_id={axis: peer}, device_id_type=MESH,
        ).start()

    def to_col(phase, landing, src, dst, far):
        base = (1 - side_c if far else side_c) * (2 * depth)

        def body(i, _):
            stem = base + 2 * lax.rem(zone_z + hop(i, depth), depth)
            ship(src, dst, phase, landing, "col", stem + 1 - core)
            ship(src, dst, phase, landing, "col", stem + core)
            return 0

        lax.fori_loop(0, depth if far else depth - 1, body, 0)
        if not far:
            ship(src, dst, phase, landing, "col", base + 2 * zone_z + 1 - core)

    def to_row(phase, landing, src, dst, far):
        base = (1 - side_r if far else side_r) * width

        def body(i, _):
            ship(src, dst, phase, landing, "row", base + lax.rem(place + hop(i, width), width))
            return 0

        lax.fori_loop(0, width if far else width - 1, body, 0)

    def to_quarter(phase, landing, src, dst, quarter, own):
        def body(i, _):
            ship(src, dst, phase, landing, "col", quarter * depth + lax.rem(lax.rem(c, depth) + depth - i, depth))
            return 0

        lax.fori_loop(1 if own else 0, depth, body, 0)

    near = lax.div(c, depth)
    order = [(1 - lax.div(near, 2)) * 2 + (1 - lax.rem(near, 2)), (1 - lax.div(near, 2)) * 2 + lax.rem(near, 2),
             lax.div(near, 2) * 2 + (1 - lax.rem(near, 2)), near]

    def arrived(phase, part):
        pltpu.make_async_copy(part, part, recv.at[phase]).wait()

    def left(phase, part):
        pltpu.make_async_copy(part, part, send.at[phase]).wait()

    for far in (True, False):
        to_col(0, 0, lambda peer: vol.at[:, sixteen(peer), :], rows0.at[c], far)
    rows0[c] = vol[:, sixteen(c), :]

    eye = one_hot(iota((BLOCK, BLOCK), 0) == iota((BLOCK, BLOCK), 1))
    anti = one_hot(iota((BLOCK, BLOCK), 0) == BLOCK - 1 - iota((BLOCK, BLOCK), 1))

    lane = iota((LINES, 128), 1)

    def table(offset):
        row = iota((256, WIN), 0) - offset
        row = jnp.where(iota((256, WIN), 0) < offset - 64, row + 256, row)
        return dot(one_hot(row == iota((256, WIN), 1)), fwd[...]).astype(BF)

    def merged(ref, start, count, offset):
        outer = jnp.where(
            iota((1, 1, LINES, 128), 3) < offset - 64, ref[pl.ds(start + 2, count)], ref[pl.ds(start, count)]
        )
        middle = ref[pl.ds(start + 1, count)]
        return jnp.concatenate([t.reshape(count * 2 * LINES, 128) for t in (outer, middle)], 1)

    def prepare(index, shifts, fractions, start, base, width):
        mine = iota((LINES, width), 1) == start + iota((LINES, width), 0)
        f = jnp.sum(jnp.where(mine, fractions, 0.0), axis=1, keepdims=True)
        k = jnp.sum(jnp.where(mine, shifts.astype(F32), 0.0), axis=1, keepdims=True)
        phase = (2.0 * np.pi / WIN) * f * lane.astype(F32)
        ramps[index, 0] = jnp.cos(phase)
        ramps[index, 1] = jnp.sin(phase)
        ramps[index, 2] = jnp.broadcast_to(k - base.astype(F32), (LINES, 128))
        offset = (-MARGIN - base) & 127
        tabs[index] = table(offset)

    def row_base(v, p):
        return jnp.minimum(srs[v, p, c * LINES], srs[v, p, c * LINES + LINES - 1])

    def col_base(v):
        return jnp.minimum(scs[v, r * LINES], scs[v, r * LINES + LINES - 1])

    for v in range(2):
        for p in range(2):
            prepare(3 * v + 2 * p, sr[v, pl.ds(p, 1), :], fr[v, pl.ds(p, 1), :], c * LINES, row_base(v, p), tile_rows)
        prepare(3 * v + 1, sc[pl.ds(v, 1), :], fc[pl.ds(v, 1), :], r * LINES, col_base(v), BLOCK)
    tabs[6] = table(jnp.int32(96))

    for part in range(2):
        flipped = dot(anti, wb[part]).astype(BF)
        for n in range(quarters):
            wbt[part, n * BLOCK : (n + 1) * BLOCK, :] = dot_nt(eye, flipped[:, n * BLOCK : (n + 1) * BLOCK]).astype(BF)

    zone[...] = jnp.zeros(zone.shape, BF)
    for v in range(2):
        ub[v, 0] = jnp.zeros((2, LINES, 128), BF)
        ub[v, col_tiles + 1] = jnp.zeros((2, LINES, 128), BF)

    pad = 14

    def shear(index, base, bits, src, count, dst, side, after):
        shift = ramps[index, 2].astype(jnp.int32)
        a = src[...].astype(F32)
        zero = jnp.zeros((1, 2, LINES, 128), F32)
        a = jnp.concatenate([a, zero], 0)
        for bit in range(bits):
            step = 2**bit
            turned = pltpu.roll(a, step, 3)
            before = jnp.concatenate([zero, turned[:-1]], 0)
            moved = jnp.where(lane >= step, turned, before)
            a = jnp.where((shift & step) != 0, moved, a)
        zone[pad : pad + count + 1] = a.astype(BF)
        first = lax.shift_right_arithmetic(-MARGIN - base, 7) + pad
        offset = (-MARGIN - base) & 127
        cosine = ramps[index, 0]
        sine = ramps[index, 1]
        group = count // 2
        for far in (True, False):
            m = (1 - side if far else side) * group
            spectrum = dot(merged(zone, first + m, group, offset), tabs[index])
            even = spectrum[:, :128].reshape(group * 2, LINES, 128)
            odd = spectrum[:, 128:].reshape(group * 2, LINES, 128)
            y = jnp.concatenate([even * cosine - odd * sine, odd * cosine + even * sine], 2)
            line = dot(y.reshape(group * 2 * LINES, 256).astype(BF), inv[...])
            dst[pl.ds(m, group)] = line.reshape(group, 2, LINES, 128).astype(BF)
            after(far)

    for v in range(2):
        if v == 0:
            arrived(0, rows0.at[pl.ds(0, nc - 1)])

        def after(far, v=v):
            to_col(3 + v, 17 + 4 * v + near, lambda peer: o1.at[v, peer], tile1.at[v, :, sixteen(c), :], far)

        shear(3 * v, row_base(v, 0), 3, rows0, col_tiles, o1.at[v], side_c, after)
        tile1[v, :, sixteen(c), :] = o1[v, c]

    def landed(landing, part, own):
        def wait(number):
            whole = part.at[:, pl.ds(0, number * LINES), :]
            pltpu.make_async_copy(whole, whole, recv.at[landing]).wait()

        wait(depth - 1 if own else depth)

    for v in range(2):
        for i, k in enumerate(order):
            spot = pl.ds(pl.multiple_of(k * BLOCK, BLOCK), BLOCK)
            landed(17 + 4 * v + k, tile1.at[v], i == 3)
            for part in range(2):
                turn1[v, k, part] = dot_nt(eye, tile1[v, part, spot, :]).astype(BF)
            for far in (True, False):
                to_row(
                    5 + v, 5 + v, lambda peer, v=v, k=k: turn1.at[v, k, :, sixteen(peer), :],
                    cols.at[v, r * quarters + k], far,
                )
            cols[v, r * quarters + k] = turn1[v, k, :, sixteen(r), :]
        for far in (True, False):
            if v == 0:
                to_col(1, 1, lambda peer: wa.at[:, sixteen(peer), :], wrow_a.at[c], far)
            else:
                to_col(2, 2, lambda peer: wbt.at[:, sixteen(peer), :], wrow_b.at[nc - 1 - c], far)
    wrow_a[c] = wa[:, sixteen(c), :]
    wrow_b[nc - 1 - c] = wbt[:, sixteen(c), :]

    for v in range(2):
        arrived(5 + v, cols.at[v, pl.ds(0, row_tiles - quarters)])

        def after(far, v=v):
            for k in order:
                to_row(
                    7 + v, 25 + 4 * v + k, lambda peer, k=k: o2.at[v, peer * quarters + k],
                    turn2.at[v, k, :, sixteen(r), :], far,
                )

        shear(3 * v + 1, col_base(v), 4, cols.at[v], row_tiles, o2.at[v], side_r, after)
        turn2[v, :, :, sixteen(r), :] = o2[v, pl.ds(r * quarters, quarters)]

    for v in range(2):
        for i, k in enumerate(order):
            spot = pl.ds(pl.multiple_of(k * BLOCK, BLOCK), BLOCK)
            arrived(25 + 4 * v + k, turn2.at[v, 0, :, pl.ds(0, BLOCK - LINES), :])
            for part in range(2):
                tile2[v, part, spot, :] = dot_nt(eye, turn2[v, k, part]).astype(BF)
            to_quarter(9 + v, 9 + v, lambda peer, v=v: tile2.at[v, :, sixteen(peer), :], rows2.at[v, c], k, i == 3)
        rows2[v, c] = tile2[v, :, sixteen(c), :]

    for v in range(2):
        wave = (wrow_a, wrow_b)[v]
        arrived(9 + v, rows2.at[v, pl.ds(0, nc - 1)])
        shear(3 * v + 2, row_base(v, 1), 3, rows2.at[v], col_tiles, rot, side_c, lambda far: None)
        arrived(1 + v, wave.at[pl.ds(0, nc - 1)])
        group = 4

        def through(g, _, v=v, wave=wave):
            m = g * group
            block = rot[pl.ds(m, group)].astype(F32)
            w = wave[pl.ds(m, group)].astype(F32)
            amplitude = jnp.exp(-ABSORB * block[:, 1])
            real = amplitude * jnp.cos(block[:, 0])
            imaginary = amplitude * jnp.sin(block[:, 0])
            ub[v, pl.ds(1 + m, group), 0] = (w[:, 0] * real - w[:, 1] * imaginary).astype(BF)
            ub[v, pl.ds(1 + m, group), 1] = (w[:, 0] * imaginary + w[:, 1] * real).astype(BF)
            return 0

        lax.fori_loop(0, col_tiles // group, through, 0)
        phase = travel_phase(trav[v], iota((1, 256), 1) & 127)
        factor_real = jnp.cos(phase)
        factor_imaginary = jnp.sin(phase)
        span = col_tiles // 2
        spot = pl.ds(pl.multiple_of(MARGIN + c * LINES, LINES), LINES)
        for far in (True, False):
            m = (side_c if far == (v == 1) else 1 - side_c) * span
            spectrum = dot(merged(ub.at[v], m, span, 96), tabs[6]).reshape(span, 2, LINES, 256)
            a, b = spectrum[:, 0], spectrum[:, 1]
            y = jnp.stack([factor_real * a - factor_imaginary * b, factor_real * b + factor_imaginary * a], 1)
            line = dot(y.reshape(span * 2 * LINES, 256).astype(BF), inv[...])
            half[v, pl.ds(m, span)] = line.reshape(span, 2, LINES, 128).astype(BF)
            if v == 0:
                to_col(11, 33 + near, lambda peer: half.at[0, peer], ext.at[0, :, spot, :], far)
            else:
                to_col(12, 37 + near, lambda peer: half.at[1, nc - 1 - peer], ext.at[1, :, spot, :], far)
        ext[v, :, spot, :] = half[v, c if v == 0 else nc - 1 - c]

    top = pl.ds(0, MARGIN)
    bottom = pl.ds(MARGIN + tile_rows, MARGIN)
    head = pl.ds(MARGIN, MARGIN)
    tail = pl.ds(tile_rows, MARGIN)

    def down(v):
        return pltpu.make_async_remote_copy(
            src_ref=ext.at[v, :, tail, :], dst_ref=ext.at[v, :, top, :], send_sem=send.at[13 + v],
            recv_sem=recv.at[13 + v], device_id={"row": lax.rem(r + 1, nr)}, device_id_type=MESH,
        )

    def up(v):
        return pltpu.make_async_remote_copy(
            src_ref=ext.at[v, :, head, :], dst_ref=ext.at[v, :, bottom, :], send_sem=send.at[15 + v],
            recv_sem=recv.at[15 + v], device_id={"row": lax.rem(r + nr - 1, nr)}, device_id_type=MESH,
        )

    for v in range(2):
        for k in range(4):

            @pl.when(near == k)
            def _(v=v, k=k):
                landed(33 + 4 * v + k, ext.at[v], True)

            @pl.when(near != k)
            def _(v=v, k=k):
                landed(33 + 4 * v + k, ext.at[v], False)

        @pl.when(r < nr - 1)
        def _(v=v):
            down(v).start()

        @pl.when(r > 0)
        def _(v=v):
            up(v).start()

        @pl.when(r == 0)
        def _(v=v):
            ext[v, :, top, :] = jnp.zeros((2, MARGIN, 128), BF)

        @pl.when(r == nr - 1)
        def _(v=v):
            ext[v, :, bottom, :] = jnp.zeros((2, MARGIN, 128), BF)

        @pl.when(r > 0)
        def _(v=v):
            down(v).wait_recv()

        @pl.when(r < nr - 1)
        def _(v=v):
            up(v).wait_recv()

        if v == 0:
            phase = travel_phase(trav[0], iota((256, 128), 0) & 127)
            factor_real = jnp.cos(phase)
            factor_imaginary = jnp.sin(phase)
            for n in range(quarters):
                window = jnp.concatenate([ext[0, part, n * BLOCK : n * BLOCK + WIN, :] for part in range(2)], 1)
                spectrum = dot(fwdt[...], window)
                a, b = spectrum[:, :128], spectrum[:, 128:]
                y = jnp.concatenate(
                    [factor_real * a - factor_imaginary * b, factor_real * b + factor_imaginary * a], 1
                ).astype(BF)
                line = dot(invt[...], y).astype(BF)
                out_a[0, n * BLOCK : (n + 1) * BLOCK, :] = line[:, :128]
                out_a[1, n * BLOCK : (n + 1) * BLOCK, :] = line[:, 128:]
        else:
            phase = travel_phase(trav[1], iota((1, 256), 1) & 127)
            factor_real = jnp.cos(phase)
            factor_imaginary = jnp.sin(phase)
            for part in range(2):
                extt[part, :, 0 : tile_rows + 2 * MARGIN] = dot_nt(anti, ext[1, part]).astype(BF)
                extt[part, :, tile_rows + 2 * MARGIN :] = jnp.zeros((BLOCK, MARGIN * 2), BF)
            for n in range(quarters):
                window = extt[:, :, n * BLOCK : (n + 2) * BLOCK].reshape(2 * BLOCK, 2 * BLOCK)
                spectrum = dot(window[:, :WIN], fwd[...])
                a, b = spectrum[:BLOCK], spectrum[BLOCK:]
                y = jnp.concatenate(
                    [factor_real * a - factor_imaginary * b, factor_real * b + factor_imaginary * a], 0
                ).astype(BF)
                line = dot(y, inv[...]).astype(BF)
                out_b[0, :, n * BLOCK : (n + 1) * BLOCK] = line[:BLOCK]
                out_b[1, :, n * BLOCK : (n + 1) * BLOCK] = line[BLOCK:]

    left(0, vol.at[:, pl.ds(0, tile_rows - LINES), :])
    left(1, wa.at[:, pl.ds(0, tile_rows - LINES), :])
    left(2, wbt.at[:, pl.ds(0, tile_rows - LINES), :])
    for v in range(2):
        left(3 + v, o1.at[v, pl.ds(0, nc - 1)])
        left(5 + v, turn1.at[v, :, :, pl.ds(0, BLOCK - LINES), :])
        left(7 + v, o2.at[v, pl.ds(0, row_tiles - quarters)])
        left(9 + v, tile2.at[v, :, pl.ds(0, tile_rows - LINES), :])
        left(11 + v, half.at[v, pl.ds(0, nc - 1)])

        @pl.when(r < nr - 1)
        def _(v=v):
            down(v).wait_send()

        @pl.when(r > 0)
        def _(v=v):
            up(v).wait_send()


def on_device(nr, nc, vol, wa, wb, sr, fr, sc, fc, trav):
    forward, inverse = real_tables()
    tile_rows = nc * LINES
    quarters = tile_rows // BLOCK
    col_tiles, row_tiles = nc, nr * quarters
    vmem = pl.BlockSpec(memory_space=pltpu.VMEM)
    smem = pl.BlockSpec(memory_space=pltpu.SMEM)
    lines = (2, LINES, 128)
    scratch = [
        pltpu.VMEM((2, tile_rows, 128), BF),
        pltpu.VMEM((col_tiles, *lines), BF),
        pltpu.VMEM((col_tiles, *lines), BF),
        pltpu.VMEM((col_tiles, *lines), BF),
        pltpu.VMEM((64, *lines), BF),
        pltpu.VMEM((2, col_tiles, *lines), BF),
        pltpu.VMEM((2, 2, tile_rows, 128), BF),
        pltpu.VMEM((2, quarters, 2, BLOCK, 128), BF),
        pltpu.VMEM((2, row_tiles, *lines), BF),
        pltpu.VMEM((2, row_tiles, *lines), BF),
        pltpu.VMEM((2, quarters, 2, BLOCK, 128), BF),
        pltpu.VMEM((2, 2, tile_rows, 128), BF),
        pltpu.VMEM((2, col_tiles, *lines), BF),
        pltpu.VMEM((col_tiles, *lines), BF),
        pltpu.VMEM((2, col_tiles + 2, *lines), BF),
        pltpu.VMEM((2, col_tiles, *lines), BF),
        pltpu.VMEM((2, 2, tile_rows + 2 * MARGIN, 128), BF),
        pltpu.VMEM((2, BLOCK, tile_rows + BLOCK), BF),
        pltpu.VMEM((6, 3, LINES, 128), F32),
        pltpu.VMEM((7, 256, 256), BF),
        pltpu.SemaphoreType.DMA((17,)),
        pltpu.SemaphoreType.DMA((41,)),
    ]
    return pl.pallas_call(
        functools.partial(kernel, nr, nc),
        out_shape=(
            jax.ShapeDtypeStruct((2, tile_rows, 128), BF),
            jax.ShapeDtypeStruct((2, 128, tile_rows), BF),
        ),
        in_specs=[vmem] * 3 + [smem] * 3 + [vmem] * 8,
        out_specs=(vmem, vmem),
        scratch_shapes=scratch,
        compiler_params=pltpu.CompilerParams(
            collective_id=0, has_side_effects=True, vmem_limit_bytes=56 * 2**20
        ),
        name="rotate_travel",
    )(
        vol, wa, wb, sr, sc, trav, sr, fr, sc, fc,
        jnp.asarray(forward, BF), jnp.asarray(inverse, BF),
        jnp.asarray(forward.T, BF), jnp.asarray(inverse.T, BF),
    )


def solution(mesh):
    nr, nc = mesh.shape["row"], mesh.shape["col"]
    return jax.shard_map(
        functools.partial(on_device, nr, nc),
        mesh=mesh,
        in_specs=(
            P(None, "row", "col"),
            P(None, "row", "col"),
            P(None, "col", "row"),
            P(None, None, "row"),
            P(None, None, "row"),
            P(None, "col"),
            P(None, "col"),
            P(),
        ),
        out_specs=(P(None, "row", "col"), P(None, "col", "row")),
        check_vma=False,
    )
```

```python
import functools

import jax
import jax.numpy as jnp
import numpy as np
from jax import lax
from jax.experimental import pallas as pl
from jax.experimental.pallas import tpu as pltpu
from jax.sharding import PartitionSpec as P

BLOCK = 128
MARGIN = 32
WIN = BLOCK + 2 * MARGIN
HALF = WIN // 2
LINES = 16
ABSORB = 0.25
MESH = pl.DeviceIdType.MESH
BF = jnp.bfloat16
F32 = jnp.float32


def real_tables():
    q = np.arange(HALF + 1)
    p = np.arange(WIN)
    angle = (2.0 * np.pi * np.mod(p[:, None] * q[None, :], WIN).astype(np.float32) / WIN).astype(np.float32)
    forward = np.zeros((WIN, 256), np.float32)
    forward[:, : HALF + 1] = np.cos(angle)
    forward[:, 129 : 128 + HALF] = np.sin(angle)[:, 1:HALF]
    target = np.arange(BLOCK) + MARGIN
    angle = (2.0 * np.pi * np.mod(q[:, None] * target[None, :], WIN).astype(np.float32) / WIN).astype(np.float32)
    weight = np.where((q == 0) | (q == HALF), 1.0, 2.0)[:, None].astype(np.float32)
    inverse = np.zeros((256, BLOCK), np.float32)
    inverse[: HALF + 1] = weight * (np.cos(angle) / WIN)
    inverse[129 : 128 + HALF] = (2.0 * np.sin(angle) / WIN)[1:HALF]
    return forward, inverse


def iota(shape, dim):
    return lax.broadcasted_iota(jnp.int32, shape, dim)


def one_hot(mask):
    return jnp.where(mask, 1.0, 0.0).astype(BF)


def dot(a, b):
    return jnp.dot(a, b, preferred_element_type=F32)


def dot_nt(a, b):
    return lax.dot_general(a, b, (((1,), (1,)), ((), ())), preferred_element_type=F32)


def cos_sin(x):
    turns = jnp.floor(x * np.float32(2.0 / np.pi) + 0.5)
    y = ((x - turns * np.float32(1.5703125)) - turns * np.float32(4.837512969970703125e-4)) - turns * np.float32(
        7.54978995489188216e-8
    )
    z = y * y
    sine = y + y * z * (np.float32(-1.6666654611e-1) + z * (np.float32(8.3321608736e-3) + z * np.float32(-1.9515295891e-4)))
    cosine = 1.0 - 0.5 * z + z * z * (
        np.float32(4.166664568298827e-2) + z * (np.float32(-1.388731625493765e-3) + z * np.float32(2.443315711809948e-5))
    )
    quarter = turns.astype(jnp.int32)
    swap = (quarter & 1) == 1
    real, imaginary = jnp.where(swap, sine, cosine), jnp.where(swap, cosine, sine)
    real = jnp.where(((quarter + 1) & 2) == 2, -real, real)
    return real, jnp.where((quarter & 2) == 2, -imaginary, imaginary)


def travel_phase(z, q):
    q = q.astype(F32)
    return (-2.0 * np.pi / (WIN * WIN)) * z * q * q


def kernel(
    nr, nc, vol_in, wa_in, wb_in, sr_in, fr_in, sc_in, fc_in, trav_in, fwd_in, inv_in, fwdt_in, invt_in,
    out_a, out_b,
    vol, wa, wb, srs, scs, trav, sr, fr, sc, fc, fwd, inv, fwdt, invt, load,
    wbt, rows0, wrow_a, wrow_b, zone, o1, tile1, turn1, cols, o2, turn2, tile2, rows2, rot, ub, half, ext,
    ramps, tabs, send, recv,
):
    r = lax.axis_index("row")
    c = lax.axis_index("col")
    tile_rows = nc * LINES
    quarters = tile_rows // BLOCK
    col_tiles = nc
    row_tiles = nr * quarters

    barrier = pltpu.get_barrier_semaphore()

    def greet_col(i, _):
        pl.semaphore_signal(barrier, inc=1, device_id={"col": lax.rem(c + i, nc)}, device_id_type=MESH)
        return 0

    def greet_row(i, _):
        pl.semaphore_signal(barrier, inc=1, device_id={"row": lax.rem(r + i, nr)}, device_id_type=MESH)
        return 0

    lax.fori_loop(1, nc, greet_col, 0)
    lax.fori_loop(1, nr, greet_row, 0)
    loads = [
        pltpu.make_async_copy(src, dst, load.at[i])
        for i, (src, dst) in enumerate([
            (vol_in, vol), (wa_in, wa), (wb_in, wb), (sr_in, srs), (sc_in, scs), (trav_in, trav), (sr_in, sr), (fr_in, fr), (sc_in, sc),
            (fc_in, fc), (fwd_in, fwd), (inv_in, inv), (fwdt_in, fwdt), (invt_in, invt),
        ])
    ]
    for copy in loads:
        copy.start()
    loads[0].wait()
    pl.semaphore_wait(barrier, nc + nr - 2)

    def sixteen(i):
        return pl.ds(pl.multiple_of(i * LINES, LINES), LINES)

    depth = nc // 4
    width = nr // 2
    zone_z, core = lax.rem(lax.div(c, 2), depth), lax.rem(c, 2)
    side_c, side_r = lax.div(c, 2 * depth), lax.div(r, width)
    place = lax.rem(r, width)

    def hops(ring):
        far = ring // 2
        return [far - (i + 1) // 2 if i % 2 else far + i // 2 for i in range(ring)]

    def ship(src, dst, phase, landing, axis, peer):
        pltpu.make_async_remote_copy(
            src_ref=src(peer), dst_ref=dst, send_sem=send.at[phase], recv_sem=recv.at[landing],
            device_id={axis: peer}, device_id_type=MESH,
        ).start()

    def to_col(phase, landing, src, dst, far):
        base = (1 - side_c if far else side_c) * (2 * depth)
        for step in hops(depth):
            stem = base + 2 * lax.rem(zone_z + step, depth)
            ship(src, dst, phase, landing, "col", stem + 1 - core)
            if far or step:
                ship(src, dst, phase, landing, "col", stem + core)

    def to_row(phase, landing, src, dst, far):
        base = (1 - side_r if far else side_r) * width
        for step in hops(width):
            if far or step:
                ship(src, dst, phase, landing, "row", base + lax.rem(place + step, width))

    def to_quarter(phase, landing, src, dst, quarter, own):
        for step in range(1 if own else 0, depth):
            peer = quarter * depth + lax.rem(lax.rem(c, depth) + depth - step, depth)
            ship(src, dst, phase, landing, "col", peer)

    near = lax.div(c, depth)
    order = [(1 - lax.div(near, 2)) * 2 + (1 - lax.rem(near, 2)), (1 - lax.div(near, 2)) * 2 + lax.rem(near, 2),
             lax.div(near, 2) * 2 + (1 - lax.rem(near, 2)), near]

    def arrived(phase, part):
        pltpu.make_async_copy(part, part, recv.at[phase]).wait()

    def left(phase, part):
        pltpu.make_async_copy(part, part, send.at[phase]).wait()

    def send_wave(v, far):
        if v == 0:
            to_col(1, 1, lambda peer: wa.at[:, sixteen(peer), :], wrow_a.at[c], far)
        else:
            to_col(2, 2, lambda peer: wbt.at[:, sixteen(peer), :], wrow_b.at[nc - 1 - c], far)

    for far in (True, False):
        to_col(0, 0, lambda peer: vol.at[:, sixteen(peer), :], rows0.at[c], far)
    for copy in loads[1:]:
        copy.wait()
    rows0[c] = vol[:, sixteen(c), :]
    wrow_a[c] = wa[:, sixteen(c), :]

    eye = one_hot(iota((BLOCK, BLOCK), 0) == iota((BLOCK, BLOCK), 1))
    anti = one_hot(iota((BLOCK, BLOCK), 0) == BLOCK - 1 - iota((BLOCK, BLOCK), 1))

    lane = iota((LINES, 128), 1)

    def table(offset):
        row = iota((256, WIN), 0) - offset
        row = jnp.where(iota((256, WIN), 0) < offset - 64, row + 256, row)
        return dot(one_hot(row == iota((256, WIN), 1)), fwd[...]).astype(BF)

    def merged(ref, start, count, offset):
        outer = jnp.where(
            iota((1, 1, LINES, 128), 3) < offset - 64, ref[pl.ds(start + 2, count)], ref[pl.ds(start, count)]
        )
        middle = ref[pl.ds(start + 1, count)]
        return jnp.concatenate([t.reshape(count * 2 * LINES, 128) for t in (outer, middle)], 1)

    def prepare(index, shifts, fractions, start, base, width):
        mine = iota((LINES, width), 1) == start + iota((LINES, width), 0)
        f = jnp.sum(jnp.where(mine, fractions, 0.0), axis=1, keepdims=True)
        k = jnp.sum(jnp.where(mine, shifts.astype(F32), 0.0), axis=1, keepdims=True)
        phase = (2.0 * np.pi / WIN) * f * lane.astype(F32)
        ramps[index, 0] = jnp.cos(phase)
        ramps[index, 1] = jnp.sin(phase)
        ramps[index, 2] = jnp.broadcast_to(k - base.astype(F32), (LINES, 128))
        offset = (-MARGIN - base) & 127
        tabs[index] = table(offset)

    def row_base(v, p):
        return jnp.minimum(srs[v, p, c * LINES], srs[v, p, c * LINES + LINES - 1])

    def col_base(v):
        return jnp.minimum(scs[v, r * LINES], scs[v, r * LINES + LINES - 1])

    for v in range(2):
        for p in range(2):
            prepare(3 * v + 2 * p, sr[v, pl.ds(p, 1), :], fr[v, pl.ds(p, 1), :], c * LINES, row_base(v, p), tile_rows)
        prepare(3 * v + 1, sc[pl.ds(v, 1), :], fc[pl.ds(v, 1), :], r * LINES, col_base(v), BLOCK)
    tabs[6] = table(jnp.int32(96))

    for part in range(2):
        flipped = dot(anti, wb[part]).astype(BF)
        for n in range(quarters):
            wbt[part, n * BLOCK : (n + 1) * BLOCK, :] = dot_nt(eye, flipped[:, n * BLOCK : (n + 1) * BLOCK]).astype(BF)

    zone[...] = jnp.zeros(zone.shape, BF)
    for v in range(2):
        ub[v, 0] = jnp.zeros((2, LINES, 128), BF)
        ub[v, col_tiles + 1] = jnp.zeros((2, LINES, 128), BF)

    pad = 14

    def shear(index, base, bits, src, count, dst, side, after):
        shift = ramps[index, 2].astype(jnp.int32)
        a = src[...].astype(F32)
        zero = jnp.zeros((1, 2, LINES, 128), F32)
        a = jnp.concatenate([a, zero], 0)
        for bit in range(bits):
            step = 2**bit
            turned = pltpu.roll(a, step, 3)
            before = jnp.concatenate([zero, turned[:-1]], 0)
            moved = jnp.where(lane >= step, turned, before)
            a = jnp.where((shift & step) != 0, moved, a)
        zone[pad : pad + count + 1] = a.astype(BF)
        first = lax.shift_right_arithmetic(-MARGIN - base, 7) + pad
        offset = (-MARGIN - base) & 127
        cosine = ramps[index, 0]
        sine = ramps[index, 1]
        group = count // 2
        for far in (True, False):
            m = (1 - side if far else side) * group
            spectrum = dot(merged(zone, first + m, group, offset), tabs[index])
            even = spectrum[:, :128].reshape(group * 2, LINES, 128)
            odd = spectrum[:, 128:].reshape(group * 2, LINES, 128)
            y = jnp.concatenate([even * cosine - odd * sine, odd * cosine + even * sine], 2)
            line = dot(y.reshape(group * 2 * LINES, 256).astype(BF), inv[...])
            dst[pl.ds(m, group)] = line.reshape(group, 2, LINES, 128).astype(BF)
            after(far)

    send_wave(0, True)
    for v in range(2):
        if v == 0:
            arrived(0, rows0.at[pl.ds(0, nc - 1)])

        def after(far, v=v):
            to_col(3 + v, 17 + 4 * v + near, lambda peer: o1.at[v, peer], tile1.at[v, :, sixteen(c), :], far)

        shear(3 * v, row_base(v, 0), 3, rows0, col_tiles, o1.at[v], side_c, after)
        tile1[v, :, sixteen(c), :] = o1[v, c]

    def landed(landing, part, own):
        def wait(number):
            whole = part.at[:, pl.ds(0, number * LINES), :]
            pltpu.make_async_copy(whole, whole, recv.at[landing]).wait()

        wait(depth - 1 if own else depth)

    def rows_to_columns(v):
        for i, k in enumerate(order):
            spot = pl.ds(pl.multiple_of(k * BLOCK, BLOCK), BLOCK)
            landed(17 + 4 * v + k, tile1.at[v], i == 3)
            for part in range(2):
                turn1[v, k, part] = dot_nt(eye, tile1[v, part, spot, :]).astype(BF)
            for far in (True, False):
                to_row(
                    5 + v, 5 + v, lambda peer: turn1.at[v, k, :, sixteen(peer), :], cols.at[v, r * quarters + k], far
                )
            cols[v, r * quarters + k] = turn1[v, k, :, sixteen(r), :]

    def shear_columns(v):
        arrived(5 + v, cols.at[v, pl.ds(0, row_tiles - quarters)])

        shear(3 * v + 1, col_base(v), 4, cols.at[v], row_tiles, o2.at[v], side_r, lambda far: None)
        for k in order:
            for far in (True, False):
                to_row(
                    7 + v, 25 + 4 * v + k, lambda peer: o2.at[v, peer * quarters + k],
                    turn2.at[v, k, :, sixteen(r), :], far,
                )
        turn2[v, :, :, sixteen(r), :] = o2[v, pl.ds(r * quarters, quarters)]

    def columns_to_rows(v):
        for i, k in enumerate(order):
            spot = pl.ds(pl.multiple_of(k * BLOCK, BLOCK), BLOCK)
            arrived(25 + 4 * v + k, turn2.at[v, 0, :, pl.ds(0, BLOCK - LINES), :])
            for part in range(2):
                tile2[v, part, spot, :] = dot_nt(eye, turn2[v, k, part]).astype(BF)
            to_quarter(9 + v, 9 + v, lambda peer: tile2.at[v, :, sixteen(peer), :], rows2.at[v, c], k, i == 3)
        rows2[v, c] = tile2[v, :, sixteen(c), :]

    wrow_b[nc - 1 - c] = wbt[:, sixteen(c), :]
    rows_to_columns(0)
    send_wave(0, False)
    send_wave(1, False)
    rows_to_columns(1)
    shear_columns(0)
    columns_to_rows(0)
    shear_columns(1)
    send_wave(1, True)
    columns_to_rows(1)

    for v in range(2):
        wave = (wrow_a, wrow_b)[v]
        arrived(9 + v, rows2.at[v, pl.ds(0, nc - 1)])
        shear(3 * v + 2, row_base(v, 1), 3, rows2.at[v], col_tiles, rot, side_c, lambda far: None)
        arrived(1 + v, wave.at[pl.ds(0, nc - 1)])
        group = 4

        def through(g, _, v=v, wave=wave):
            m = g * group
            block = rot[pl.ds(m, group)].astype(F32)
            w = wave[pl.ds(m, group)].astype(F32)
            amplitude = jnp.exp(-ABSORB * block[:, 1])
            cosine, sine = cos_sin(block[:, 0])
            real = amplitude * cosine
            imaginary = amplitude * sine
            ub[v, pl.ds(1 + m, group), 0] = (w[:, 0] * real - w[:, 1] * imaginary).astype(BF)
            ub[v, pl.ds(1 + m, group), 1] = (w[:, 0] * imaginary + w[:, 1] * real).astype(BF)
            return 0

        lax.fori_loop(0, col_tiles // group, through, 0)
        phase = travel_phase(trav[v], iota((1, 256), 1) & 127)
        factor_real = jnp.cos(phase)
        factor_imaginary = jnp.sin(phase)
        span = col_tiles // 2
        spot = pl.ds(pl.multiple_of(MARGIN + c * LINES, LINES), LINES)
        for far in (True, False):
            m = (side_c if far == (v == 1) else 1 - side_c) * span
            spectrum = dot(merged(ub.at[v], m, span, 96), tabs[6]).reshape(span, 2, LINES, 256)
            a, b = spectrum[:, 0], spectrum[:, 1]
            y = jnp.stack([factor_real * a - factor_imaginary * b, factor_real * b + factor_imaginary * a], 1)
            line = dot(y.reshape(span * 2 * LINES, 256).astype(BF), inv[...])
            half[v, pl.ds(m, span)] = line.reshape(span, 2, LINES, 128).astype(BF)
            if v == 0:
                to_col(11, 33 + near, lambda peer: half.at[0, peer], ext.at[0, :, spot, :], far)
            else:
                to_col(12, 37 + near, lambda peer: half.at[1, nc - 1 - peer], ext.at[1, :, spot, :], far)
        ext[v, :, spot, :] = half[v, c if v == 0 else nc - 1 - c]

    top = pl.ds(0, MARGIN)
    bottom = pl.ds(MARGIN + tile_rows, MARGIN)
    head = pl.ds(MARGIN, MARGIN)
    tail = pl.ds(tile_rows, MARGIN)

    def down(v):
        return pltpu.make_async_remote_copy(
            src_ref=ext.at[v, :, tail, :], dst_ref=ext.at[v, :, top, :], send_sem=send.at[13 + v],
            recv_sem=recv.at[13 + v], device_id={"row": lax.rem(r + 1, nr)}, device_id_type=MESH,
        )

    def up(v):
        return pltpu.make_async_remote_copy(
            src_ref=ext.at[v, :, head, :], dst_ref=ext.at[v, :, bottom, :], send_sem=send.at[15 + v],
            recv_sem=recv.at[15 + v], device_id={"row": lax.rem(r + nr - 1, nr)}, device_id_type=MESH,
        )

    phase = travel_phase(trav[0], iota((256, 128), 0) & 127)
    down_real, down_imaginary = jnp.cos(phase), jnp.sin(phase)
    phase = travel_phase(trav[1], iota((1, 256), 1) & 127)
    along_real, along_imaginary = jnp.cos(phase), jnp.sin(phase)

    def finish(v, n):
        rows = slice(n * BLOCK, n * BLOCK + WIN)
        spot = slice(n * BLOCK, (n + 1) * BLOCK)
        if v == 0:
            window = jnp.concatenate([ext[0, part, rows, :] for part in range(2)], 1)
            spectrum = dot(fwdt[...], window)
            a, b = spectrum[:, :128], spectrum[:, 128:]
            y = jnp.concatenate([down_real * a - down_imaginary * b, down_real * b + down_imaginary * a], 1)
            line = dot(invt[...], y.astype(BF)).astype(BF)
            out_a[0, spot, :] = line[:, :128]
            out_a[1, spot, :] = line[:, 128:]
        else:
            window = jnp.concatenate([dot_nt(anti, ext[1, part, rows, :]).astype(BF) for part in range(2)], 0)
            spectrum = dot(window, fwd[...])
            a, b = spectrum[:BLOCK], spectrum[BLOCK:]
            y = jnp.concatenate([along_real * a - along_imaginary * b, along_real * b + along_imaginary * a], 0)
            line = dot(y.astype(BF), inv[...]).astype(BF)
            out_b[0, :, spot] = line[:BLOCK]
            out_b[1, :, spot] = line[BLOCK:]

    for v in range(2):
        for k in (0, quarters - 1, *range(1, quarters - 1)):

            @pl.when(near == k)
            def _(v=v, k=k):
                landed(33 + 4 * v + k, ext.at[v], True)

            @pl.when(near != k)
            def _(v=v, k=k):
                landed(33 + 4 * v + k, ext.at[v], False)

            if k == 0:

                @pl.when(r > 0)
                def _(v=v):
                    up(v).start()

                @pl.when(r == 0)
                def _(v=v):
                    ext[v, :, top, :] = jnp.zeros((2, MARGIN, 128), BF)

            if k == quarters - 1:

                @pl.when(r < nr - 1)
                def _(v=v):
                    down(v).start()

                @pl.when(r == nr - 1)
                def _(v=v):
                    ext[v, :, bottom, :] = jnp.zeros((2, MARGIN, 128), BF)

        for n in range(1, quarters - 1):
            finish(v, n)

        @pl.when(r > 0)
        def _(v=v):
            down(v).wait_recv()

        finish(v, 0)

        @pl.when(r < nr - 1)
        def _(v=v):
            up(v).wait_recv()

        finish(v, quarters - 1)

    left(0, vol.at[:, pl.ds(0, tile_rows - LINES), :])
    left(1, wa.at[:, pl.ds(0, tile_rows - LINES), :])
    left(2, wbt.at[:, pl.ds(0, tile_rows - LINES), :])
    for v in range(2):
        left(3 + v, o1.at[v, pl.ds(0, nc - 1)])
        left(5 + v, turn1.at[v, :, :, pl.ds(0, BLOCK - LINES), :])
        left(7 + v, o2.at[v, pl.ds(0, row_tiles - quarters)])
        left(9 + v, tile2.at[v, :, pl.ds(0, tile_rows - LINES), :])
        left(11 + v, half.at[v, pl.ds(0, nc - 1)])

        @pl.when(r < nr - 1)
        def _(v=v):
            down(v).wait_send()

        @pl.when(r > 0)
        def _(v=v):
            up(v).wait_send()


def on_device(nr, nc, vol, wa, wb, sr, fr, sc, fc, trav):
    forward, inverse = real_tables()
    tile_rows = nc * LINES
    quarters = tile_rows // BLOCK
    col_tiles, row_tiles = nc, nr * quarters
    anywhere = pl.BlockSpec(memory_space=pl.ANY)
    lines = (2, LINES, 128)
    scratch = [
        pltpu.VMEM((2, tile_rows, 128), BF),
        pltpu.VMEM((2, tile_rows, 128), BF),
        pltpu.VMEM((2, BLOCK, tile_rows), BF),
        pltpu.SMEM(sr.shape, jnp.int32),
        pltpu.SMEM(sc.shape, jnp.int32),
        pltpu.SMEM(trav.shape, F32),
        pltpu.VMEM(sr.shape, jnp.int32),
        pltpu.VMEM(fr.shape, F32),
        pltpu.VMEM(sc.shape, jnp.int32),
        pltpu.VMEM(fc.shape, F32),
        pltpu.VMEM((WIN, 256), BF),
        pltpu.VMEM((256, BLOCK), BF),
        pltpu.VMEM((256, WIN), BF),
        pltpu.VMEM((BLOCK, 256), BF),
        pltpu.SemaphoreType.DMA((14,)),
        pltpu.VMEM((2, tile_rows, 128), BF),
        pltpu.VMEM((col_tiles, *lines), BF),
        pltpu.VMEM((col_tiles, *lines), BF),
        pltpu.VMEM((col_tiles, *lines), BF),
        pltpu.VMEM((64, *lines), BF),
        pltpu.VMEM((2, col_tiles, *lines), BF),
        pltpu.VMEM((2, 2, tile_rows, 128), BF),
        pltpu.VMEM((2, quarters, 2, BLOCK, 128), BF),
        pltpu.VMEM((2, row_tiles, *lines), BF),
        pltpu.VMEM((2, row_tiles, *lines), BF),
        pltpu.VMEM((2, quarters, 2, BLOCK, 128), BF),
        pltpu.VMEM((2, 2, tile_rows, 128), BF),
        pltpu.VMEM((2, col_tiles, *lines), BF),
        pltpu.VMEM((col_tiles, *lines), BF),
        pltpu.VMEM((2, col_tiles + 2, *lines), BF),
        pltpu.VMEM((2, col_tiles, *lines), BF),
        pltpu.VMEM((2, 2, tile_rows + 2 * MARGIN, 128), BF),
        pltpu.VMEM((6, 3, LINES, 128), F32),
        pltpu.VMEM((7, 256, 256), BF),
        pltpu.SemaphoreType.DMA((17,)),
        pltpu.SemaphoreType.DMA((41,)),
    ]
    result = pl.pallas_call(
        functools.partial(kernel, nr, nc),
        out_shape=(
            pltpu.VMEM((2, tile_rows, 128), BF),
            pltpu.VMEM((2, 128, tile_rows), BF),
        ),
        in_specs=[pl.BlockSpec(memory_space=pltpu.HBM)] * 12,
        out_specs=(pl.BlockSpec(memory_space=pltpu.VMEM),) * 2,
        scratch_shapes=scratch,
        compiler_params=pltpu.CompilerParams(
            collective_id=0, has_side_effects=True, vmem_limit_bytes=65994752
        ),
        name="rotate_travel",
    )(
        vol, wa, wb, sr, fr, sc, fc, trav,
        jnp.asarray(forward, BF), jnp.asarray(inverse, BF),
        jnp.asarray(forward.T, BF), jnp.asarray(inverse.T, BF),
    )
    return pl.pallas_call(
        hand_over,
        out_shape=tuple(jax.ShapeDtypeStruct(x.shape, x.dtype) for x in result),
        in_specs=[anywhere] * 2,
        out_specs=(anywhere, anywhere),
        scratch_shapes=[pltpu.SemaphoreType.DMA((2,))],
        compiler_params=pltpu.CompilerParams(vmem_limit_bytes=2 * 2**20),
        name="hand_over",
    )(*result)


def hand_over(a, b, out_a, out_b, sem):
    given = [pltpu.make_async_copy(a, out_a, sem.at[0]), pltpu.make_async_copy(b, out_b, sem.at[1])]
    for copy in given:
        copy.start()
    for copy in given:
        copy.wait()


def solution(mesh):
    nr, nc = mesh.shape["row"], mesh.shape["col"]
    return jax.shard_map(
        functools.partial(on_device, nr, nc),
        mesh=mesh,
        in_specs=(
            P(None, "row", "col"),
            P(None, "row", "col"),
            P(None, "col", "row"),
            P(None, None, "row"),
            P(None, None, "row"),
            P(None, "col"),
            P(None, "col"),
            P(),
        ),
        out_specs=(P(None, "row", "col"), P(None, "col", "row")),
        check_vma=False,
    )
```

```python
import functools

import jax
import jax.numpy as jnp
import numpy as np
from jax import lax
from jax.experimental import pallas as pl
from jax.experimental.pallas import tpu as pltpu
from jax.sharding import PartitionSpec as P

BLOCK = 128
MARGIN = 32
WIN = BLOCK + 2 * MARGIN
HALF = WIN // 2
LINES = 16
ABSORB = 0.25
MESH = pl.DeviceIdType.MESH
BF = jnp.bfloat16
F32 = jnp.float32


def real_tables():
    q = np.arange(HALF + 1)
    p = np.arange(WIN)
    angle = (2.0 * np.pi * np.mod(p[:, None] * q[None, :], WIN).astype(np.float32) / WIN).astype(np.float32)
    forward = np.zeros((WIN, 256), np.float32)
    forward[:, : HALF + 1] = np.cos(angle)
    forward[:, 129 : 128 + HALF] = np.sin(angle)[:, 1:HALF]
    target = np.arange(BLOCK) + MARGIN
    angle = (2.0 * np.pi * np.mod(q[:, None] * target[None, :], WIN).astype(np.float32) / WIN).astype(np.float32)
    weight = np.where((q == 0) | (q == HALF), 1.0, 2.0)[:, None].astype(np.float32)
    inverse = np.zeros((256, BLOCK), np.float32)
    inverse[: HALF + 1] = weight * (np.cos(angle) / WIN)
    inverse[129 : 128 + HALF] = (2.0 * np.sin(angle) / WIN)[1:HALF]
    return forward, inverse


def iota(shape, dim):
    return lax.broadcasted_iota(jnp.int32, shape, dim)


def one_hot(mask):
    return jnp.where(mask, 1.0, 0.0).astype(BF)


def dot(a, b):
    return jnp.dot(a, b, preferred_element_type=F32)


def dot_nt(a, b):
    return lax.dot_general(a, b, (((1,), (1,)), ((), ())), preferred_element_type=F32)


def cos_sin(x):
    turns = jnp.floor(x * np.float32(2.0 / np.pi) + 0.5)
    y = ((x - turns * np.float32(1.5703125)) - turns * np.float32(4.837512969970703125e-4)) - turns * np.float32(
        7.54978995489188216e-8
    )
    z = y * y
    sine = y + y * z * (np.float32(-1.6666654611e-1) + z * (np.float32(8.3321608736e-3) + z * np.float32(-1.9515295891e-4)))
    cosine = 1.0 - 0.5 * z + z * z * (
        np.float32(4.166664568298827e-2) + z * (np.float32(-1.388731625493765e-3) + z * np.float32(2.443315711809948e-5))
    )
    quarter = turns.astype(jnp.int32)
    swap = (quarter & 1) == 1
    real, imaginary = jnp.where(swap, sine, cosine), jnp.where(swap, cosine, sine)
    real = jnp.where(((quarter + 1) & 2) == 2, -real, real)
    return real, jnp.where((quarter & 2) == 2, -imaginary, imaginary)


def travel_phase(z, q):
    q = q.astype(F32)
    return (-2.0 * np.pi / (WIN * WIN)) * z * q * q


def kernel(
    nr, nc, vol_in, wa_in, wb_in, sr_in, fr_in, sc_in, fc_in, trav_in, fwd_in, inv_in, fwdt_in, invt_in,
    out_a, out_b,
    vol, wa, wb, srs, scs, trav, sr, fr, sc, fc, fwd, inv, fwdt, invt, load,
    wbt, rows0, wrow_a, wrow_b, zone, o1, tile1, turn1, cols, o2, turn2, tile2, rows2, rot, ub, half, ext,
    ramps, tabs, send, recv,
):
    r = lax.axis_index("row")
    c = lax.axis_index("col")
    tile_rows = nc * LINES
    quarters = tile_rows // BLOCK
    col_tiles = nc
    row_tiles = nr * quarters

    barrier = pltpu.get_barrier_semaphore()

    def greet_col(i, _):
        pl.semaphore_signal(barrier, inc=1, device_id={"col": lax.rem(c + i, nc)}, device_id_type=MESH)
        return 0

    def greet_row(i, _):
        pl.semaphore_signal(barrier, inc=1, device_id={"row": lax.rem(r + i, nr)}, device_id_type=MESH)
        return 0

    lax.fori_loop(1, nc, greet_col, 0)
    lax.fori_loop(1, nr, greet_row, 0)
    loads = [
        pltpu.make_async_copy(src, dst, load.at[i])
        for i, (src, dst) in enumerate([
            (vol_in, vol), (wa_in, wa), (wb_in, wb), (sr_in, srs), (sc_in, scs), (trav_in, trav), (sr_in, sr), (fr_in, fr), (sc_in, sc),
            (fc_in, fc), (fwd_in, fwd), (inv_in, inv), (fwdt_in, fwdt), (invt_in, invt),
        ])
    ]
    for copy in loads:
        copy.start()
    loads[0].wait()
    pl.semaphore_wait(barrier, nc + nr - 2)

    def sixteen(i):
        return pl.ds(pl.multiple_of(i * LINES, LINES), LINES)

    depth = nc // 4
    width = nr // 2
    zone_z, core = lax.rem(lax.div(c, 2), depth), lax.rem(c, 2)
    side_c, side_r = lax.div(c, 2 * depth), lax.div(r, width)
    place = lax.rem(r, width)

    def hops(ring):
        far = ring // 2
        return [far - (i + 1) // 2 if i % 2 else far + i // 2 for i in range(ring)]

    def ship(src, dst, phase, landing, axis, peer):
        pltpu.make_async_remote_copy(
            src_ref=src(peer), dst_ref=dst, send_sem=send.at[phase], recv_sem=recv.at[landing],
            device_id={axis: peer}, device_id_type=MESH,
        ).start()

    def to_col(phase, landing, src, dst, far):
        base = (1 - side_c if far else side_c) * (2 * depth)
        for step in hops(depth):
            stem = base + 2 * lax.rem(zone_z + step, depth)
            ship(src, dst, phase, landing, "col", stem + 1 - core)
            if far or step:
                ship(src, dst, phase, landing, "col", stem + core)

    def to_row(phase, landing, src, dst, far):
        base = (1 - side_r if far else side_r) * width
        for step in hops(width):
            if far or step:
                ship(src, dst, phase, landing, "row", base + lax.rem(place + step, width))

    def to_quarter(phase, landing, src, dst, quarter, own):
        for step in range(1 if own else 0, depth):
            peer = quarter * depth + lax.rem(lax.rem(c, depth) + depth - step, depth)
            ship(src, dst, phase, landing, "col", peer)

    near = lax.div(c, depth)
    order = [(1 - lax.div(near, 2)) * 2 + (1 - lax.rem(near, 2)), (1 - lax.div(near, 2)) * 2 + lax.rem(near, 2),
             lax.div(near, 2) * 2 + (1 - lax.rem(near, 2)), near]

    def arrived(phase, part):
        pltpu.make_async_copy(part, part, recv.at[phase]).wait()

    def left(phase, part):
        pltpu.make_async_copy(part, part, send.at[phase]).wait()

    def send_wave(v, far):
        if v == 0:
            to_col(1, 1, lambda peer: wa.at[:, sixteen(peer), :], wrow_a.at[c], far)
        else:
            to_col(2, 2, lambda peer: wbt.at[:, sixteen(peer), :], wrow_b.at[nc - 1 - c], far)

    for far in (True, False):
        to_col(0, 0, lambda peer: vol.at[:, sixteen(peer), :], rows0.at[c], far)
    for copy in loads[1:]:
        copy.wait()
    rows0[c] = vol[:, sixteen(c), :]
    wrow_a[c] = wa[:, sixteen(c), :]

    eye = one_hot(iota((BLOCK, BLOCK), 0) == iota((BLOCK, BLOCK), 1))
    anti = one_hot(iota((BLOCK, BLOCK), 0) == BLOCK - 1 - iota((BLOCK, BLOCK), 1))

    lane = iota((LINES, 128), 1)

    def table(offset):
        row = iota((256, WIN), 0) - offset
        row = jnp.where(iota((256, WIN), 0) < offset - 64, row + 256, row)
        return dot(one_hot(row == iota((256, WIN), 1)), fwd[...]).astype(BF)

    def merged(ref, start, count, offset):
        outer = jnp.where(
            iota((1, 1, LINES, 128), 3) < offset - 64, ref[pl.ds(start + 2, count)], ref[pl.ds(start, count)]
        )
        middle = ref[pl.ds(start + 1, count)]
        return jnp.concatenate([t.reshape(count * 2 * LINES, 128) for t in (outer, middle)], 1)

    def prepare(index, shifts, fractions, start, base, width):
        mine = iota((LINES, width), 1) == start + iota((LINES, width), 0)
        f = jnp.sum(jnp.where(mine, fractions, 0.0), axis=1, keepdims=True)
        k = jnp.sum(jnp.where(mine, shifts.astype(F32), 0.0), axis=1, keepdims=True)
        phase = (2.0 * np.pi / WIN) * f * lane.astype(F32)
        ramps[index, 0] = jnp.cos(phase)
        ramps[index, 1] = jnp.sin(phase)
        ramps[index, 2] = jnp.broadcast_to(k - base.astype(F32), (LINES, 128))
        offset = (-MARGIN - base) & 127
        tabs[index] = table(offset)

    def row_base(v, p):
        return jnp.minimum(srs[v, p, c * LINES], srs[v, p, c * LINES + LINES - 1])

    def col_base(v):
        return jnp.minimum(scs[v, r * LINES], scs[v, r * LINES + LINES - 1])

    for v in range(2):
        for p in range(2):
            prepare(3 * v + 2 * p, sr[v, pl.ds(p, 1), :], fr[v, pl.ds(p, 1), :], c * LINES, row_base(v, p), tile_rows)
        prepare(3 * v + 1, sc[pl.ds(v, 1), :], fc[pl.ds(v, 1), :], r * LINES, col_base(v), BLOCK)
    tabs[6] = table(jnp.int32(96))

    for part in range(2):
        flipped = dot(anti, wb[part]).astype(BF)
        for n in range(quarters):
            wbt[part, n * BLOCK : (n + 1) * BLOCK, :] = dot_nt(eye, flipped[:, n * BLOCK : (n + 1) * BLOCK]).astype(BF)

    zone[...] = jnp.zeros(zone.shape, BF)
    for v in range(2):
        ub[v, 0] = jnp.zeros((2, LINES, 128), BF)
        ub[v, col_tiles + 1] = jnp.zeros((2, LINES, 128), BF)

    pad = 14

    def shear(index, base, bits, src, count, dst, side, after):
        shift = ramps[index, 2].astype(jnp.int32)
        a = src[...].astype(F32)
        zero = jnp.zeros((1, 2, LINES, 128), F32)
        a = jnp.concatenate([a, zero], 0)
        for bit in range(bits):
            step = 2**bit
            turned = pltpu.roll(a, step, 3)
            before = jnp.concatenate([zero, turned[:-1]], 0)
            moved = jnp.where(lane >= step, turned, before)
            a = jnp.where((shift & step) != 0, moved, a)
        zone[pad : pad + count + 1] = a.astype(BF)
        first = lax.shift_right_arithmetic(-MARGIN - base, 7) + pad
        offset = (-MARGIN - base) & 127
        cosine = ramps[index, 0]
        sine = ramps[index, 1]
        group = count // 2
        for far in (True, False):
            m = (1 - side if far else side) * group
            spectrum = dot(merged(zone, first + m, group, offset), tabs[index])
            even = spectrum[:, :128].reshape(group * 2, LINES, 128)
            odd = spectrum[:, 128:].reshape(group * 2, LINES, 128)
            y = jnp.concatenate([even * cosine - odd * sine, odd * cosine + even * sine], 2)
            line = dot(y.reshape(group * 2 * LINES, 256).astype(BF), inv[...])
            dst[pl.ds(m, group)] = line.reshape(group, 2, LINES, 128).astype(BF)
            after(far)

    send_wave(0, True)
    send_wave(1, True)
    for v in range(2):
        if v == 0:
            arrived(0, rows0.at[pl.ds(0, nc - 1)])

        def after(far, v=v):
            to_col(3 + v, 17 + 4 * v + near, lambda peer: o1.at[v, peer], tile1.at[v, :, sixteen(c), :], far)

        shear(3 * v, row_base(v, 0), 3, rows0, col_tiles, o1.at[v], side_c, after)
        tile1[v, :, sixteen(c), :] = o1[v, c]

    def landed(landing, part, own):
        def wait(number):
            whole = part.at[:, pl.ds(0, number * LINES), :]
            pltpu.make_async_copy(whole, whole, recv.at[landing]).wait()

        wait(depth - 1 if own else depth)

    def rows_to_columns(v, which=(0, 1, 2, 3)):
        for i in which:
            k = order[i]
            spot = pl.ds(pl.multiple_of(k * BLOCK, BLOCK), BLOCK)
            landed(17 + 4 * v + k, tile1.at[v], i == 3)
            for part in range(2):
                turn1[v, k, part] = dot_nt(eye, tile1[v, part, spot, :]).astype(BF)
            for far in (True, False):
                to_row(
                    5 + v, 5 + v, lambda peer: turn1.at[v, k, :, sixteen(peer), :], cols.at[v, r * quarters + k], far
                )
            cols[v, r * quarters + k] = turn1[v, k, :, sixteen(r), :]

    def shear_columns(v):
        arrived(5 + v, cols.at[v, pl.ds(0, row_tiles - quarters)])

        shear(3 * v + 1, col_base(v), 4, cols.at[v], row_tiles, o2.at[v], side_r, lambda far: None)
        for k in order:
            for far in (True, False):
                to_row(
                    7 + v, 25 + 4 * v + k, lambda peer: o2.at[v, peer * quarters + k],
                    turn2.at[v, k, :, sixteen(r), :], far,
                )
        turn2[v, :, :, sixteen(r), :] = o2[v, pl.ds(r * quarters, quarters)]

    def columns_to_rows(v, which=(0, 1, 2, 3)):
        for i in which:
            k = order[i]
            spot = pl.ds(pl.multiple_of(k * BLOCK, BLOCK), BLOCK)
            arrived(25 + 4 * v + k, turn2.at[v, 0, :, pl.ds(0, BLOCK - LINES), :])
            for part in range(2):
                tile2[v, part, spot, :] = dot_nt(eye, turn2[v, k, part]).astype(BF)
            to_quarter(9 + v, 9 + v, lambda peer: tile2.at[v, :, sixteen(peer), :], rows2.at[v, c], k, i == 3)
        if which[-1] == 3:
            rows2[v, c] = tile2[v, :, sixteen(c), :]

    wrow_b[nc - 1 - c] = wbt[:, sixteen(c), :]
    send_wave(0, False)
    send_wave(1, False)
    rows_to_columns(0)
    rows_to_columns(1)
    shear_columns(0)
    shear_columns(1)
    columns_to_rows(0)
    columns_to_rows(1)

    for v in range(2):
        wave = (wrow_a, wrow_b)[v]
        arrived(9 + v, rows2.at[v, pl.ds(0, nc - 1)])
        shear(3 * v + 2, row_base(v, 1), 3, rows2.at[v], col_tiles, rot, side_c, lambda far: None)
        arrived(1 + v, wave.at[pl.ds(0, nc - 1)])
        group = 4

        def through(g, _, v=v, wave=wave):
            m = g * group
            block = rot[pl.ds(m, group)].astype(F32)
            w = wave[pl.ds(m, group)].astype(F32)
            amplitude = jnp.exp(-ABSORB * block[:, 1])
            cosine, sine = cos_sin(block[:, 0])
            real = amplitude * cosine
            imaginary = amplitude * sine
            ub[v, pl.ds(1 + m, group), 0] = (w[:, 0] * real - w[:, 1] * imaginary).astype(BF)
            ub[v, pl.ds(1 + m, group), 1] = (w[:, 0] * imaginary + w[:, 1] * real).astype(BF)
            return 0

        lax.fori_loop(0, col_tiles // group, through, 0)
        phase = travel_phase(trav[v], iota((1, 256), 1) & 127)
        factor_real = jnp.cos(phase)
        factor_imaginary = jnp.sin(phase)
        span = col_tiles // 2
        spot = pl.ds(pl.multiple_of(MARGIN + c * LINES, LINES), LINES)
        for far in (True, False):
            m = (side_c if far == (v == 1) else 1 - side_c) * span
            spectrum = dot(merged(ub.at[v], m, span, 96), tabs[6]).reshape(span, 2, LINES, 256)
            a, b = spectrum[:, 0], spectrum[:, 1]
            y = jnp.stack([factor_real * a - factor_imaginary * b, factor_real * b + factor_imaginary * a], 1)
            line = dot(y.reshape(span * 2 * LINES, 256).astype(BF), inv[...])
            half[v, pl.ds(m, span)] = line.reshape(span, 2, LINES, 128).astype(BF)
            if v == 0:
                to_col(11, 33 + near, lambda peer: half.at[0, peer], ext.at[0, :, spot, :], far)
            else:
                to_col(12, 37 + near, lambda peer: half.at[1, nc - 1 - peer], ext.at[1, :, spot, :], far)
        ext[v, :, spot, :] = half[v, c if v == 0 else nc - 1 - c]

    top = pl.ds(0, MARGIN)
    bottom = pl.ds(MARGIN + tile_rows, MARGIN)
    head = pl.ds(MARGIN, MARGIN)
    tail = pl.ds(tile_rows, MARGIN)

    def down(v):
        return pltpu.make_async_remote_copy(
            src_ref=ext.at[v, :, tail, :], dst_ref=ext.at[v, :, top, :], send_sem=send.at[13 + v],
            recv_sem=recv.at[13 + v], device_id={"row": lax.rem(r + 1, nr)}, device_id_type=MESH,
        )

    def up(v):
        return pltpu.make_async_remote_copy(
            src_ref=ext.at[v, :, head, :], dst_ref=ext.at[v, :, bottom, :], send_sem=send.at[15 + v],
            recv_sem=recv.at[15 + v], device_id={"row": lax.rem(r + nr - 1, nr)}, device_id_type=MESH,
        )

    phase = travel_phase(trav[0], iota((256, 128), 0) & 127)
    down_real, down_imaginary = jnp.cos(phase), jnp.sin(phase)
    phase = travel_phase(trav[1], iota((1, 256), 1) & 127)
    along_real, along_imaginary = jnp.cos(phase), jnp.sin(phase)

    def finish(v, blocks):
        count = len(blocks)
        rows = [slice(n * BLOCK, n * BLOCK + WIN) for n in blocks]
        spots = [slice(n * BLOCK, (n + 1) * BLOCK) for n in blocks]
        if v == 0:
            window = jnp.concatenate([ext[0, part, at, :] for part in range(2) for at in rows], 1)
            spectrum = dot(fwdt[...], window)
            a, b = spectrum[:, : count * 128], spectrum[:, count * 128 :]
            real, imaginary = (jnp.concatenate([x] * count, 1) for x in (down_real, down_imaginary))
            y = jnp.concatenate([real * a - imaginary * b, real * b + imaginary * a], 1)
            line = dot(invt[...], y.astype(BF)).astype(BF)
            for part in range(2):
                for i, at in enumerate(spots):
                    out_a[part, at, :] = line[:, (part * count + i) * 128 : (part * count + i + 1) * 128]
        else:
            window = jnp.concatenate(
                [dot_nt(anti, ext[1, part, at, :]).astype(BF) for part in range(2) for at in rows], 0
            )
            spectrum = dot(window, fwd[...])
            a, b = spectrum[: count * BLOCK], spectrum[count * BLOCK :]
            y = jnp.concatenate([along_real * a - along_imaginary * b, along_real * b + along_imaginary * a], 0)
            line = dot(y.astype(BF), inv[...]).astype(BF)
            for part in range(2):
                for i, at in enumerate(spots):
                    out_b[part, :, at] = line[(part * count + i) * BLOCK : (part * count + i + 1) * BLOCK]

    for v in range(2):
        for k in (0, quarters - 1, *range(1, quarters - 1)):

            @pl.when(near == k)
            def _(v=v, k=k):
                landed(33 + 4 * v + k, ext.at[v], True)

            @pl.when(near != k)
            def _(v=v, k=k):
                landed(33 + 4 * v + k, ext.at[v], False)

            if k == 0:

                @pl.when(r > 0)
                def _(v=v):
                    up(v).start()

                @pl.when(r == 0)
                def _(v=v):
                    ext[v, :, top, :] = jnp.zeros((2, MARGIN, 128), BF)

            if k == quarters - 1:

                @pl.when(r < nr - 1)
                def _(v=v):
                    down(v).start()

                @pl.when(r == nr - 1)
                def _(v=v):
                    ext[v, :, bottom, :] = jnp.zeros((2, MARGIN, 128), BF)

        finish(v, tuple(range(1, quarters - 1)))

        @pl.when(r > 0)
        def _(v=v):
            down(v).wait_recv()

        @pl.when(r < nr - 1)
        def _(v=v):
            up(v).wait_recv()

        finish(v, (0, quarters - 1))

    left(0, vol.at[:, pl.ds(0, tile_rows - LINES), :])
    left(1, wa.at[:, pl.ds(0, tile_rows - LINES), :])
    left(2, wbt.at[:, pl.ds(0, tile_rows - LINES), :])
    for v in range(2):
        left(3 + v, o1.at[v, pl.ds(0, nc - 1)])
        left(5 + v, turn1.at[v, :, :, pl.ds(0, BLOCK - LINES), :])
        left(7 + v, o2.at[v, pl.ds(0, row_tiles - quarters)])
        left(9 + v, tile2.at[v, :, pl.ds(0, tile_rows - LINES), :])
        left(11 + v, half.at[v, pl.ds(0, nc - 1)])

        @pl.when(r < nr - 1)
        def _(v=v):
            down(v).wait_send()

        @pl.when(r > 0)
        def _(v=v):
            up(v).wait_send()


def on_device(nr, nc, vol, wa, wb, sr, fr, sc, fc, trav):
    forward, inverse = real_tables()
    tile_rows = nc * LINES
    quarters = tile_rows // BLOCK
    col_tiles, row_tiles = nc, nr * quarters
    anywhere = pl.BlockSpec(memory_space=pl.ANY)
    lines = (2, LINES, 128)
    scratch = [
        pltpu.VMEM((2, tile_rows, 128), BF),
        pltpu.VMEM((2, tile_rows, 128), BF),
        pltpu.VMEM((2, BLOCK, tile_rows), BF),
        pltpu.SMEM(sr.shape, jnp.int32),
        pltpu.SMEM(sc.shape, jnp.int32),
        pltpu.SMEM(trav.shape, F32),
        pltpu.VMEM(sr.shape, jnp.int32),
        pltpu.VMEM(fr.shape, F32),
        pltpu.VMEM(sc.shape, jnp.int32),
        pltpu.VMEM(fc.shape, F32),
        pltpu.VMEM((WIN, 256), BF),
        pltpu.VMEM((256, BLOCK), BF),
        pltpu.VMEM((256, WIN), BF),
        pltpu.VMEM((BLOCK, 256), BF),
        pltpu.SemaphoreType.DMA((14,)),
        pltpu.VMEM((2, tile_rows, 128), BF),
        pltpu.VMEM((col_tiles, *lines), BF),
        pltpu.VMEM((col_tiles, *lines), BF),
        pltpu.VMEM((col_tiles, *lines), BF),
        pltpu.VMEM((64, *lines), BF),
        pltpu.VMEM((2, col_tiles, *lines), BF),
        pltpu.VMEM((2, 2, tile_rows, 128), BF),
        pltpu.VMEM((2, quarters, 2, BLOCK, 128), BF),
        pltpu.VMEM((2, row_tiles, *lines), BF),
        pltpu.VMEM((2, row_tiles, *lines), BF),
        pltpu.VMEM((2, quarters, 2, BLOCK, 128), BF),
        pltpu.VMEM((2, 2, tile_rows, 128), BF),
        pltpu.VMEM((2, col_tiles, *lines), BF),
        pltpu.VMEM((col_tiles, *lines), BF),
        pltpu.VMEM((2, col_tiles + 2, *lines), BF),
        pltpu.VMEM((2, col_tiles, *lines), BF),
        pltpu.VMEM((2, 2, tile_rows + 2 * MARGIN, 128), BF),
        pltpu.VMEM((6, 3, LINES, 128), F32),
        pltpu.VMEM((7, 256, 256), BF),
        pltpu.SemaphoreType.DMA((17,)),
        pltpu.SemaphoreType.DMA((41,)),
    ]
    result = pl.pallas_call(
        functools.partial(kernel, nr, nc),
        out_shape=(
            pltpu.VMEM((2, tile_rows, 128), BF),
            pltpu.VMEM((2, 128, tile_rows), BF),
        ),
        in_specs=[pl.BlockSpec(memory_space=pltpu.HBM)] * 12,
        out_specs=(pl.BlockSpec(memory_space=pltpu.VMEM),) * 2,
        scratch_shapes=scratch,
        compiler_params=pltpu.CompilerParams(
            collective_id=0, has_side_effects=True, vmem_limit_bytes=65994752
        ),
        name="rotate_travel",
    )(
        vol, wa, wb, sr, fr, sc, fc, trav,
        jnp.asarray(forward, BF), jnp.asarray(inverse, BF),
        jnp.asarray(forward.T, BF), jnp.asarray(inverse.T, BF),
    )
    return pl.pallas_call(
        hand_over,
        out_shape=tuple(jax.ShapeDtypeStruct(x.shape, x.dtype) for x in result),
        in_specs=[anywhere] * 2,
        out_specs=(anywhere, anywhere),
        scratch_shapes=[pltpu.SemaphoreType.DMA((2,))],
        compiler_params=pltpu.CompilerParams(vmem_limit_bytes=2 * 2**20),
        name="hand_over",
    )(*result)


def hand_over(a, b, out_a, out_b, sem):
    given = [pltpu.make_async_copy(a, out_a, sem.at[0]), pltpu.make_async_copy(b, out_b, sem.at[1])]
    for copy in given:
        copy.start()
    for copy in given:
        copy.wait()


def solution(mesh):
    nr, nc = mesh.shape["row"], mesh.shape["col"]
    return jax.shard_map(
        functools.partial(on_device, nr, nc),
        mesh=mesh,
        in_specs=(
            P(None, "row", "col"),
            P(None, "row", "col"),
            P(None, "col", "row"),
            P(None, None, "row"),
            P(None, None, "row"),
            P(None, "col"),
            P(None, "col"),
            P(),
        ),
        out_specs=(P(None, "row", "col"), P(None, "col", "row")),
        check_vma=False,
    )
```

```python
import functools

import jax
import jax.numpy as jnp
import numpy as np
from jax import lax
from jax.experimental import pallas as pl
from jax.experimental.pallas import tpu as pltpu
from jax.sharding import PartitionSpec as P

BLOCK = 128
MARGIN = 32
WIN = BLOCK + 2 * MARGIN
HALF = WIN // 2
LINES = 16
ABSORB = 0.25
MESH = pl.DeviceIdType.MESH
BF = jnp.bfloat16
F32 = jnp.float32


def real_tables():
    q = np.arange(HALF + 1)
    p = np.arange(WIN)
    angle = (2.0 * np.pi * np.mod(p[:, None] * q[None, :], WIN).astype(np.float32) / WIN).astype(np.float32)
    forward = np.zeros((WIN, 256), np.float32)
    forward[:, : HALF + 1] = np.cos(angle)
    forward[:, 129 : 128 + HALF] = np.sin(angle)[:, 1:HALF]
    target = np.arange(BLOCK) + MARGIN
    angle = (2.0 * np.pi * np.mod(q[:, None] * target[None, :], WIN).astype(np.float32) / WIN).astype(np.float32)
    weight = np.where((q == 0) | (q == HALF), 1.0, 2.0)[:, None].astype(np.float32)
    inverse = np.zeros((256, BLOCK), np.float32)
    inverse[: HALF + 1] = weight * (np.cos(angle) / WIN)
    inverse[129 : 128 + HALF] = (2.0 * np.sin(angle) / WIN)[1:HALF]
    return forward, inverse


def iota(shape, dim):
    return lax.broadcasted_iota(jnp.int32, shape, dim)


def one_hot(mask):
    return jnp.where(mask, 1.0, 0.0).astype(BF)


def dot(a, b):
    return jnp.dot(a, b, preferred_element_type=F32)


def dot_nt(a, b):
    return lax.dot_general(a, b, (((1,), (1,)), ((), ())), preferred_element_type=F32)


def cos_sin(x):
    turns = jnp.floor(x * np.float32(2.0 / np.pi) + 0.5)
    y = ((x - turns * np.float32(1.5703125)) - turns * np.float32(4.837512969970703125e-4)) - turns * np.float32(
        7.54978995489188216e-8
    )
    z = y * y
    sine = y + y * z * (np.float32(-1.6666654611e-1) + z * (np.float32(8.3321608736e-3) + z * np.float32(-1.9515295891e-4)))
    cosine = 1.0 - 0.5 * z + z * z * (
        np.float32(4.166664568298827e-2) + z * (np.float32(-1.388731625493765e-3) + z * np.float32(2.443315711809948e-5))
    )
    quarter = turns.astype(jnp.int32)
    swap = (quarter & 1) == 1
    real, imaginary = jnp.where(swap, sine, cosine), jnp.where(swap, cosine, sine)
    real = jnp.where(((quarter + 1) & 2) == 2, -real, real)
    return real, jnp.where((quarter & 2) == 2, -imaginary, imaginary)


def travel_phase(z, q):
    q = q.astype(F32)
    return (-2.0 * np.pi / (WIN * WIN)) * z * q * q


def kernel(
    nr, nc, vol_in, wa_in, wb_in, sr_in, fr_in, sc_in, fc_in, trav_in, fwd_in, inv_in, fwdt_in, invt_in,
    out_a, out_b,
    vol, wa, wb, srs, scs, trav, sr, fr, sc, fc, fwd, inv, fwdt, invt, load,
    wbt, rows0, wrow_a, wrow_b, zone, o1, tile1, turn1, cols, o2, turn2, tile2, rows2, rot, ub, half, ext,
    ramps, tabs, send, recv,
):
    r = lax.axis_index("row")
    c = lax.axis_index("col")
    tile_rows = nc * LINES
    quarters = tile_rows // BLOCK
    col_tiles = nc
    row_tiles = nr * quarters

    barrier = pltpu.get_barrier_semaphore()

    for i in sorted(range(1, nc), key=lambda i: min(i // 2 % (nc // 4), nc // 4 - i // 2 % (nc // 4)), reverse=True):
        pl.semaphore_signal(barrier, inc=1, device_id={"col": lax.rem(c + i, nc)}, device_id_type=MESH)
    for i in range(1, nr):
        pl.semaphore_signal(barrier, inc=1, device_id={"row": lax.rem(r + i, nr)}, device_id_type=MESH)
    loads = [
        pltpu.make_async_copy(src, dst, load.at[i])
        for i, (src, dst) in enumerate([
            (vol_in, vol), (wa_in, wa), (wb_in, wb), (sr_in, srs), (sc_in, scs), (trav_in, trav), (sr_in, sr), (fr_in, fr), (sc_in, sc),
            (fc_in, fc), (fwd_in, fwd), (inv_in, inv), (fwdt_in, fwdt), (invt_in, invt),
        ])
    ]
    for copy in loads:
        copy.start()
    loads[0].wait()
    pl.semaphore_wait(barrier, nc + nr - 2)

    def sixteen(i):
        return pl.ds(pl.multiple_of(i * LINES, LINES), LINES)

    depth = nc // 4
    width = nr // 2
    zone_z, core = lax.rem(lax.div(c, 2), depth), lax.rem(c, 2)
    side_c, side_r = lax.div(c, 2 * depth), lax.div(r, width)
    place = lax.rem(r, width)

    def hops(ring):
        far = ring // 2
        return [far - (i + 1) // 2 if i % 2 else far + i // 2 for i in range(ring)]

    def ship(src, dst, phase, landing, axis, peer):
        pltpu.make_async_remote_copy(
            src_ref=src(peer), dst_ref=dst, send_sem=send.at[phase], recv_sem=recv.at[landing],
            device_id={axis: peer}, device_id_type=MESH,
        ).start()

    def to_col(phase, landing, src, dst, far):
        base = (1 - side_c if far else side_c) * (2 * depth)
        for step in hops(depth):
            stem = base + 2 * lax.rem(zone_z + step, depth)
            ship(src, dst, phase, landing, "col", stem + 1 - core)
            if far or step:
                ship(src, dst, phase, landing, "col", stem + core)

    def to_row(phase, landing, src, dst, far):
        base = (1 - side_r if far else side_r) * width
        for step in hops(width):
            if far or step:
                ship(src, dst, phase, landing, "row", base + lax.rem(place + step, width))

    def to_quarter(phase, landing, src, dst, quarter, order, own):
        chips = depth // 2
        for step in order:
            stem = quarter * depth + 2 * lax.rem(zone_z + step, chips)
            ship(src, dst, phase, landing, "col", stem + 1 - core)
            if step or not own:
                ship(src, dst, phase, landing, "col", stem + core)

    near = lax.div(c, depth)
    strip = jnp.where(c < 2, 0, jnp.where(c >= nc - 2, 1, 2 + near))
    order = [(1 - lax.div(near, 2)) * 2 + (1 - lax.rem(near, 2)), (1 - lax.div(near, 2)) * 2 + lax.rem(near, 2),
             lax.div(near, 2) * 2 + (1 - lax.rem(near, 2)), near]

    def arrived(phase, part):
        pltpu.make_async_copy(part, part, recv.at[phase]).wait()

    def left(phase, part):
        pltpu.make_async_copy(part, part, send.at[phase]).wait()

    def send_wave(v, far):
        if v == 0:
            to_col(1, 1, lambda peer: wa.at[:, sixteen(peer), :], wrow_a.at[c], far)
        else:
            to_col(2, 2, lambda peer: wbt.at[:, sixteen(peer), :], wrow_b.at[nc - 1 - c], far)

    for far in (True, False):
        to_col(0, 0, lambda peer: vol.at[:, sixteen(peer), :], rows0.at[c], far)
    for copy in loads[1:]:
        copy.wait()
    rows0[c] = vol[:, sixteen(c), :]
    wrow_a[c] = wa[:, sixteen(c), :]

    eye = one_hot(iota((BLOCK, BLOCK), 0) == iota((BLOCK, BLOCK), 1))
    anti = one_hot(iota((BLOCK, BLOCK), 0) == BLOCK - 1 - iota((BLOCK, BLOCK), 1))

    lane = iota((LINES, 128), 1)

    def table(offset):
        row = iota((256, WIN), 0) - offset
        row = jnp.where(iota((256, WIN), 0) < offset - 64, row + 256, row)
        return dot(one_hot(row == iota((256, WIN), 1)), fwd[...]).astype(BF)

    def merged(ref, start, count, offset):
        outer = jnp.where(
            iota((1, 1, LINES, 128), 3) < offset - 64, ref[pl.ds(start + 2, count)], ref[pl.ds(start, count)]
        )
        middle = ref[pl.ds(start + 1, count)]
        return jnp.concatenate([t.reshape(count * 2 * LINES, 128) for t in (outer, middle)], 1)

    def prepare(index, shifts, fractions, start, base, width):
        mine = iota((LINES, width), 1) == start + iota((LINES, width), 0)
        f = jnp.sum(jnp.where(mine, fractions, 0.0), axis=1, keepdims=True)
        k = jnp.sum(jnp.where(mine, shifts.astype(F32), 0.0), axis=1, keepdims=True)
        phase = (2.0 * np.pi / WIN) * f * lane.astype(F32)
        ramps[index, 0] = jnp.cos(phase)
        ramps[index, 1] = jnp.sin(phase)
        ramps[index, 2] = jnp.broadcast_to(k - base.astype(F32), (LINES, 128))
        offset = (-MARGIN - base) & 127
        tabs[index] = table(offset)

    def row_base(v, p):
        return jnp.minimum(srs[v, p, c * LINES], srs[v, p, c * LINES + LINES - 1])

    def col_base(v):
        return jnp.minimum(scs[v, r * LINES], scs[v, r * LINES + LINES - 1])

    for v in range(2):
        for p in range(2):
            prepare(3 * v + 2 * p, sr[v, pl.ds(p, 1), :], fr[v, pl.ds(p, 1), :], c * LINES, row_base(v, p), tile_rows)
        prepare(3 * v + 1, sc[pl.ds(v, 1), :], fc[pl.ds(v, 1), :], r * LINES, col_base(v), BLOCK)
    tabs[6] = table(jnp.int32(96))

    for part in range(2):
        flipped = dot(anti, wb[part]).astype(BF)
        for n in range(quarters):
            wbt[part, n * BLOCK : (n + 1) * BLOCK, :] = dot_nt(eye, flipped[:, n * BLOCK : (n + 1) * BLOCK]).astype(BF)

    zone[...] = jnp.zeros(zone.shape, BF)
    for v in range(2):
        ub[v, 0] = jnp.zeros((2, LINES, 128), BF)
        ub[v, col_tiles + 1] = jnp.zeros((2, LINES, 128), BF)

    pad = 14

    def shear(index, base, bits, src, count, dst, side, after):
        shift = ramps[index, 2].astype(jnp.int32)
        a = src[...].astype(F32)
        zero = jnp.zeros((1, 2, LINES, 128), F32)
        a = jnp.concatenate([a, zero], 0)
        for bit in range(bits):
            step = 2**bit
            turned = pltpu.roll(a, step, 3)
            before = jnp.concatenate([zero, turned[:-1]], 0)
            moved = jnp.where(lane >= step, turned, before)
            a = jnp.where((shift & step) != 0, moved, a)
        zone[pad : pad + count + 1] = a.astype(BF)
        first = lax.shift_right_arithmetic(-MARGIN - base, 7) + pad
        offset = (-MARGIN - base) & 127
        cosine = ramps[index, 0]
        sine = ramps[index, 1]
        group = count // 2
        for far in (True, False):
            m = (1 - side if far else side) * group
            spectrum = dot(merged(zone, first + m, group, offset), tabs[index])
            even = spectrum[:, :128].reshape(group * 2, LINES, 128)
            odd = spectrum[:, 128:].reshape(group * 2, LINES, 128)
            y = jnp.concatenate([even * cosine - odd * sine, odd * cosine + even * sine], 2)
            line = dot(y.reshape(group * 2 * LINES, 256).astype(BF), inv[...])
            dst[pl.ds(m, group)] = line.reshape(group, 2, LINES, 128).astype(BF)
            after(far)

    send_wave(0, True)
    send_wave(1, True)
    for v in range(2):
        if v == 0:
            arrived(0, rows0.at[pl.ds(0, nc - 1)])

        def after(far, v=v):
            to_col(3 + v, 17 + 4 * v + near, lambda peer: o1.at[v, peer], tile1.at[v, :, sixteen(c), :], far)

        shear(3 * v, row_base(v, 0), 3, rows0, col_tiles, o1.at[v], side_c, after)
        tile1[v, :, sixteen(c), :] = o1[v, c]

    def collected(landing, part, number):
        whole = part.at[:, pl.ds(0, number * LINES), :]
        pltpu.make_async_copy(whole, whole, recv.at[landing]).wait()

    def landed(landing, part, own):
        collected(landing, part, depth - 1 if own else depth)

    def rows_to_columns(v, which=(0, 1, 2, 3)):
        for i in which:
            k = order[i]
            spot = pl.ds(pl.multiple_of(k * BLOCK, BLOCK), BLOCK)
            landed(17 + 4 * v + k, tile1.at[v], i == 3)
            for part in range(2):
                turn1[v, k, part] = dot_nt(eye, tile1[v, part, spot, :]).astype(BF)
            for far in (True, False):
                to_row(
                    5 + v, 5 + v, lambda peer: turn1.at[v, k, :, sixteen(peer), :], cols.at[v, r * quarters + k], far
                )
            cols[v, r * quarters + k] = turn1[v, k, :, sixteen(r), :]

    def shear_columns(v):
        arrived(5 + v, cols.at[v, pl.ds(0, row_tiles - quarters)])

        shear(3 * v + 1, col_base(v), 4, cols.at[v], row_tiles, o2.at[v], side_r, lambda far: None)
        for k in order:
            for far in (True, False):
                to_row(
                    7 + v, 25 + 4 * v + k, lambda peer: o2.at[v, peer * quarters + k],
                    turn2.at[v, k, :, sixteen(r), :], far,
                )
        turn2[v, :, :, sixteen(r), :] = o2[v, pl.ds(r * quarters, quarters)]

    def columns_to_rows(v, which=(0, 1, 2, 3)):
        for i in which:
            k = order[i]
            spot = pl.ds(pl.multiple_of(k * BLOCK, BLOCK), BLOCK)
            arrived(25 + 4 * v + k, turn2.at[v, 0, :, pl.ds(0, BLOCK - LINES), :])
            for part in range(2):
                tile2[v, part, spot, :] = dot_nt(eye, turn2[v, k, part]).astype(BF)
            to_quarter(9 + v, 9 + v, lambda peer: tile2.at[v, :, sixteen(peer), :], rows2.at[v, c], k, (2, 1, 3, 0) if i % 2 else (0, 1, 3, 2), i == 3)
        if which[-1] == 3:
            rows2[v, c] = tile2[v, :, sixteen(c), :]

    wrow_b[nc - 1 - c] = wbt[:, sixteen(c), :]
    send_wave(0, False)
    send_wave(1, False)
    rows_to_columns(0)
    rows_to_columns(1)
    shear_columns(0)
    shear_columns(1)
    columns_to_rows(0)
    columns_to_rows(1)

    for v in range(2):
        wave = (wrow_a, wrow_b)[v]
        arrived(9 + v, rows2.at[v, pl.ds(0, nc - 1)])
        shear(3 * v + 2, row_base(v, 1), 3, rows2.at[v], col_tiles, rot, side_c, lambda far: None)
        arrived(1 + v, wave.at[pl.ds(0, nc - 1)])
        group = 4

        def through(g, _, v=v, wave=wave):
            m = g * group
            block = rot[pl.ds(m, group)].astype(F32)
            w = wave[pl.ds(m, group)].astype(F32)
            amplitude = jnp.exp(-ABSORB * block[:, 1])
            cosine, sine = cos_sin(block[:, 0])
            real = amplitude * cosine
            imaginary = amplitude * sine
            ub[v, pl.ds(1 + m, group), 0] = (w[:, 0] * real - w[:, 1] * imaginary).astype(BF)
            ub[v, pl.ds(1 + m, group), 1] = (w[:, 0] * imaginary + w[:, 1] * real).astype(BF)
            return 0

        lax.fori_loop(0, col_tiles // group, through, 0)
        phase = travel_phase(trav[v], iota((1, 256), 1) & 127)
        factor_real = jnp.cos(phase)
        factor_imaginary = jnp.sin(phase)
        span = col_tiles // 2
        spot = pl.ds(pl.multiple_of(MARGIN + c * LINES, LINES), LINES)
        for far in (True, False):
            m = (side_c if far == (v == 1) else 1 - side_c) * span
            spectrum = dot(merged(ub.at[v], m, span, 96), tabs[6]).reshape(span, 2, LINES, 256)
            a, b = spectrum[:, 0], spectrum[:, 1]
            y = jnp.stack([factor_real * a - factor_imaginary * b, factor_real * b + factor_imaginary * a], 1)
            line = dot(y.reshape(span * 2 * LINES, 256).astype(BF), inv[...])
            half[v, pl.ds(m, span)] = line.reshape(span, 2, LINES, 128).astype(BF)
            if v == 0:
                to_col(11, 33 + strip, lambda peer: half.at[0, peer], ext.at[0, :, spot, :], far)
            else:
                to_col(12, 39 + strip, lambda peer: half.at[1, nc - 1 - peer], ext.at[1, :, spot, :], far)
        ext[v, :, spot, :] = half[v, c if v == 0 else nc - 1 - c]

    top = pl.ds(0, MARGIN)
    bottom = pl.ds(MARGIN + tile_rows, MARGIN)
    head = pl.ds(MARGIN, MARGIN)
    tail = pl.ds(tile_rows, MARGIN)

    def down(v):
        return pltpu.make_async_remote_copy(
            src_ref=ext.at[v, :, tail, :], dst_ref=ext.at[v, :, top, :], send_sem=send.at[13 + v],
            recv_sem=recv.at[13 + v], device_id={"row": lax.rem(r + 1, nr)}, device_id_type=MESH,
        )

    def up(v):
        return pltpu.make_async_remote_copy(
            src_ref=ext.at[v, :, head, :], dst_ref=ext.at[v, :, bottom, :], send_sem=send.at[15 + v],
            recv_sem=recv.at[15 + v], device_id={"row": lax.rem(r + nr - 1, nr)}, device_id_type=MESH,
        )

    phase = travel_phase(trav[0], iota((256, 128), 0) & 127)
    down_real, down_imaginary = jnp.cos(phase), jnp.sin(phase)
    phase = travel_phase(trav[1], iota((1, 256), 1) & 127)
    along_real, along_imaginary = jnp.cos(phase), jnp.sin(phase)

    def finish(v, blocks):
        count = len(blocks)
        rows = [slice(n * BLOCK, n * BLOCK + WIN) for n in blocks]
        spots = [slice(n * BLOCK, (n + 1) * BLOCK) for n in blocks]
        if v == 0:
            window = jnp.concatenate([ext[0, part, at, :] for part in range(2) for at in rows], 1)
            spectrum = dot(fwdt[...], window)
            a, b = spectrum[:, : count * 128], spectrum[:, count * 128 :]
            real, imaginary = (jnp.concatenate([x] * count, 1) for x in (down_real, down_imaginary))
            y = jnp.concatenate([real * a - imaginary * b, real * b + imaginary * a], 1)
            line = dot(invt[...], y.astype(BF)).astype(BF)
            for part in range(2):
                for i, at in enumerate(spots):
                    out_a[part, at, :] = line[:, (part * count + i) * 128 : (part * count + i + 1) * 128]
        else:
            window = jnp.concatenate(
                [dot_nt(anti, ext[1, part, at, :]).astype(BF) for part in range(2) for at in rows], 0
            )
            spectrum = dot(window, fwd[...])
            a, b = spectrum[: count * BLOCK], spectrum[count * BLOCK :]
            y = jnp.concatenate([along_real * a - along_imaginary * b, along_real * b + along_imaginary * a], 0)
            line = dot(y.astype(BF), inv[...]).astype(BF)
            for part in range(2):
                for i, at in enumerate(spots):
                    out_b[part, :, at] = line[(part * count + i) * BLOCK : (part * count + i + 1) * BLOCK]

    counts = [2, 2, depth - 2] + [depth] * (quarters - 2) + [depth - 2]
    for v in range(2):
        for k in range(quarters + 2):

            @pl.when(strip == k)
            def _(v=v, k=k):
                collected(33 + 6 * v + k, ext.at[v], counts[k] - 1)

            @pl.when(strip != k)
            def _(v=v, k=k):
                collected(33 + 6 * v + k, ext.at[v], counts[k])

            if k == 0:

                @pl.when(r > 0)
                def _(v=v):
                    up(v).start()

                @pl.when(r == 0)
                def _(v=v):
                    ext[v, :, top, :] = jnp.zeros((2, MARGIN, 128), BF)

            if k == 1:

                @pl.when(r < nr - 1)
                def _(v=v):
                    down(v).start()

                @pl.when(r == nr - 1)
                def _(v=v):
                    ext[v, :, bottom, :] = jnp.zeros((2, MARGIN, 128), BF)

        finish(v, tuple(range(1, quarters - 1)))

        @pl.when(r > 0)
        def _(v=v):
            down(v).wait_recv()

        @pl.when(r < nr - 1)
        def _(v=v):
            up(v).wait_recv()

        finish(v, (0, quarters - 1))

    left(0, vol.at[:, pl.ds(0, tile_rows - LINES), :])
    left(1, wa.at[:, pl.ds(0, tile_rows - LINES), :])
    left(2, wbt.at[:, pl.ds(0, tile_rows - LINES), :])
    for v in range(2):
        left(3 + v, o1.at[v, pl.ds(0, nc - 1)])
        left(5 + v, turn1.at[v, :, :, pl.ds(0, BLOCK - LINES), :])
        left(7 + v, o2.at[v, pl.ds(0, row_tiles - quarters)])
        left(9 + v, tile2.at[v, :, pl.ds(0, tile_rows - LINES), :])
        left(11 + v, half.at[v, pl.ds(0, nc - 1)])

        @pl.when(r < nr - 1)
        def _(v=v):
            down(v).wait_send()

        @pl.when(r > 0)
        def _(v=v):
            up(v).wait_send()


def on_device(nr, nc, vol, wa, wb, sr, fr, sc, fc, trav):
    forward, inverse = real_tables()
    tile_rows = nc * LINES
    quarters = tile_rows // BLOCK
    col_tiles, row_tiles = nc, nr * quarters
    anywhere = pl.BlockSpec(memory_space=pl.ANY)
    lines = (2, LINES, 128)
    scratch = [
        pltpu.VMEM((2, tile_rows, 128), BF),
        pltpu.VMEM((2, tile_rows, 128), BF),
        pltpu.VMEM((2, BLOCK, tile_rows), BF),
        pltpu.SMEM(sr.shape, jnp.int32),
        pltpu.SMEM(sc.shape, jnp.int32),
        pltpu.SMEM(trav.shape, F32),
        pltpu.VMEM(sr.shape, jnp.int32),
        pltpu.VMEM(fr.shape, F32),
        pltpu.VMEM(sc.shape, jnp.int32),
        pltpu.VMEM(fc.shape, F32),
        pltpu.VMEM((WIN, 256), BF),
        pltpu.VMEM((256, BLOCK), BF),
        pltpu.VMEM((256, WIN), BF),
        pltpu.VMEM((BLOCK, 256), BF),
        pltpu.SemaphoreType.DMA((14,)),
        pltpu.VMEM((2, tile_rows, 128), BF),
        pltpu.VMEM((col_tiles, *lines), BF),
        pltpu.VMEM((col_tiles, *lines), BF),
        pltpu.VMEM((col_tiles, *lines), BF),
        pltpu.VMEM((64, *lines), BF),
        pltpu.VMEM((2, col_tiles, *lines), BF),
        pltpu.VMEM((2, 2, tile_rows, 128), BF),
        pltpu.VMEM((2, quarters, 2, BLOCK, 128), BF),
        pltpu.VMEM((2, row_tiles, *lines), BF),
        pltpu.VMEM((2, row_tiles, *lines), BF),
        pltpu.VMEM((2, quarters, 2, BLOCK, 128), BF),
        pltpu.VMEM((2, 2, tile_rows, 128), BF),
        pltpu.VMEM((2, col_tiles, *lines), BF),
        pltpu.VMEM((col_tiles, *lines), BF),
        pltpu.VMEM((2, col_tiles + 2, *lines), BF),
        pltpu.VMEM((2, col_tiles, *lines), BF),
        pltpu.VMEM((2, 2, tile_rows + 2 * MARGIN, 128), BF),
        pltpu.VMEM((6, 3, LINES, 128), F32),
        pltpu.VMEM((7, 256, 256), BF),
        pltpu.SemaphoreType.DMA((17,)),
        pltpu.SemaphoreType.DMA((45,)),
    ]
    result = pl.pallas_call(
        functools.partial(kernel, nr, nc),
        out_shape=(
            pltpu.VMEM((2, tile_rows, 128), BF),
            pltpu.VMEM((2, 128, tile_rows), BF),
        ),
        in_specs=[pl.BlockSpec(memory_space=pltpu.HBM)] * 12,
        out_specs=(pl.BlockSpec(memory_space=pltpu.VMEM),) * 2,
        scratch_shapes=scratch,
        compiler_params=pltpu.CompilerParams(
            collective_id=0, has_side_effects=True, vmem_limit_bytes=65994752
        ),
        name="rotate_travel",
    )(
        vol, wa, wb, sr, fr, sc, fc, trav,
        jnp.asarray(forward, BF), jnp.asarray(inverse, BF),
        jnp.asarray(forward.T, BF), jnp.asarray(inverse.T, BF),
    )
    return pl.pallas_call(
        hand_over,
        out_shape=tuple(jax.ShapeDtypeStruct(x.shape, x.dtype) for x in result),
        in_specs=[anywhere] * 2,
        out_specs=(anywhere, anywhere),
        scratch_shapes=[pltpu.SemaphoreType.DMA((2,))],
        compiler_params=pltpu.CompilerParams(vmem_limit_bytes=2 * 2**20),
        name="hand_over",
    )(*result)


def hand_over(a, b, out_a, out_b, sem):
    given = [pltpu.make_async_copy(a, out_a, sem.at[0]), pltpu.make_async_copy(b, out_b, sem.at[1])]
    for copy in given:
        copy.start()
    for copy in given:
        copy.wait()


def solution(mesh):
    nr, nc = mesh.shape["row"], mesh.shape["col"]
    return jax.shard_map(
        functools.partial(on_device, nr, nc),
        mesh=mesh,
        in_specs=(
            P(None, "row", "col"),
            P(None, "row", "col"),
            P(None, "col", "row"),
            P(None, None, "row"),
            P(None, None, "row"),
            P(None, "col"),
            P(None, "col"),
            P(),
        ),
        out_specs=(P(None, "row", "col"), P(None, "col", "row")),
        check_vma=False,
    )
```

```python
import functools

import jax
import jax.numpy as jnp
import numpy as np
from jax import lax
from jax.experimental import pallas as pl
from jax.experimental.pallas import tpu as pltpu
from jax.sharding import PartitionSpec as P

BLOCK = 128
MARGIN = 32
WIN = BLOCK + 2 * MARGIN
HALF = WIN // 2
LINES = 16
ABSORB = 0.25
MESH = pl.DeviceIdType.MESH
BF = jnp.bfloat16
F32 = jnp.float32


def real_tables():
    q = np.arange(HALF + 1)
    p = np.arange(WIN)
    angle = (2.0 * np.pi * np.mod(p[:, None] * q[None, :], WIN).astype(np.float32) / WIN).astype(np.float32)
    forward = np.zeros((WIN, 256), np.float32)
    forward[:, : HALF + 1] = np.cos(angle)
    forward[:, 129 : 128 + HALF] = np.sin(angle)[:, 1:HALF]
    target = np.arange(BLOCK) + MARGIN
    angle = (2.0 * np.pi * np.mod(q[:, None] * target[None, :], WIN).astype(np.float32) / WIN).astype(np.float32)
    weight = np.where((q == 0) | (q == HALF), 1.0, 2.0)[:, None].astype(np.float32)
    inverse = np.zeros((256, BLOCK), np.float32)
    inverse[: HALF + 1] = weight * (np.cos(angle) / WIN)
    inverse[129 : 128 + HALF] = (2.0 * np.sin(angle) / WIN)[1:HALF]
    return forward, inverse


def iota(shape, dim):
    return lax.broadcasted_iota(jnp.int32, shape, dim)


def one_hot(mask):
    return jnp.where(mask, 1.0, 0.0).astype(BF)


def dot(a, b):
    return jnp.dot(a, b, preferred_element_type=F32)


def dot_nt(a, b):
    return lax.dot_general(a, b, (((1,), (1,)), ((), ())), preferred_element_type=F32)


def cos_sin(x):
    turns = jnp.floor(x * np.float32(2.0 / np.pi) + 0.5)
    y = ((x - turns * np.float32(1.5703125)) - turns * np.float32(4.837512969970703125e-4)) - turns * np.float32(
        7.54978995489188216e-8
    )
    z = y * y
    sine = y + y * z * (np.float32(-1.6666654611e-1) + z * (np.float32(8.3321608736e-3) + z * np.float32(-1.9515295891e-4)))
    cosine = 1.0 - 0.5 * z + z * z * (
        np.float32(4.166664568298827e-2) + z * (np.float32(-1.388731625493765e-3) + z * np.float32(2.443315711809948e-5))
    )
    quarter = turns.astype(jnp.int32)
    swap = (quarter & 1) == 1
    real, imaginary = jnp.where(swap, sine, cosine), jnp.where(swap, cosine, sine)
    real = jnp.where(((quarter + 1) & 2) == 2, -real, real)
    return real, jnp.where((quarter & 2) == 2, -imaginary, imaginary)


def travel_phase(z, q):
    q = q.astype(F32)
    return (-2.0 * np.pi / (WIN * WIN)) * z * q * q


def kernel(
    nr, nc, vol_in, wa_in, wb_in, sr_in, fr_in, sc_in, fc_in, trav_in, fwd_in, inv_in, fwdt_in, invt_in,
    out_a, out_b,
    vol, wa, wb, srs, scs, trav, sr, fr, sc, fc, fwd, inv, fwdt, invt, load,
    wbt, rows0, wrow_a, wrow_b, zone, o1, tile1, turn1, cols, o2, turn2, tile2, rows2, rot, ub, half, ext,
    ramps, tabs, send, recv,
):
    r = lax.axis_index("row")
    c = lax.axis_index("col")
    tile_rows = nc * LINES
    quarters = tile_rows // BLOCK
    col_tiles = nc
    row_tiles = nr * quarters

    barrier = pltpu.get_barrier_semaphore()

    for i in sorted(range(1, nc), key=lambda i: min(i // 2 % (nc // 4), nc // 4 - i // 2 % (nc // 4)), reverse=True):
        pl.semaphore_signal(barrier, inc=1, device_id={"col": lax.rem(c + i, nc)}, device_id_type=MESH)
    for i in range(1, nr):
        pl.semaphore_signal(barrier, inc=1, device_id={"row": lax.rem(r + i, nr)}, device_id_type=MESH)
    loads = [
        pltpu.make_async_copy(src, dst, load.at[i])
        for i, (src, dst) in enumerate([
            (vol_in, vol), (wa_in, wa), (wb_in, wb), (sr_in, srs), (sc_in, scs), (trav_in, trav), (sr_in, sr), (fr_in, fr), (sc_in, sc),
            (fc_in, fc), (fwd_in, fwd), (inv_in, inv), (fwdt_in, fwdt), (invt_in, invt),
        ])
    ]
    for copy in loads:
        copy.start()
    loads[0].wait()
    pl.semaphore_wait(barrier, nc + nr - 2)

    def sixteen(i):
        return pl.ds(pl.multiple_of(i * LINES, LINES), LINES)

    depth = nc // 4
    width = nr // 2
    zone_z, core = lax.rem(lax.div(c, 2), depth), lax.rem(c, 2)
    side_c, side_r = lax.div(c, 2 * depth), lax.div(r, width)
    place = lax.rem(r, width)

    def hops(ring):
        far = ring // 2
        return [far - (i + 1) // 2 if i % 2 else far + i // 2 for i in range(ring)]

    def ship(src, dst, phase, landing, axis, peer):
        pltpu.make_async_remote_copy(
            src_ref=src(peer), dst_ref=dst, send_sem=send.at[phase], recv_sem=recv.at[landing],
            device_id={axis: peer}, device_id_type=MESH,
        ).start()

    def to_col(phase, landing, src, dst, far):
        base = (1 - side_c if far else side_c) * (2 * depth)
        for step in hops(depth):
            stem = base + 2 * lax.rem(zone_z + step, depth)
            ship(src, dst, phase, landing, "col", stem + 1 - core)
            if far or step:
                ship(src, dst, phase, landing, "col", stem + core)

    def to_row(phase, landing, src, dst, far):
        base = (1 - side_r if far else side_r) * width
        for step in hops(width):
            if far or step:
                ship(src, dst, phase, landing, "row", base + lax.rem(place + step, width))

    def to_quarter(phase, landing, src, dst, quarter, order, own):
        chips = depth // 2
        for step in order:
            stem = quarter * depth + 2 * lax.rem(zone_z + step, chips)
            ship(src, dst, phase, landing, "col", stem + 1 - core)
            if step or not own:
                ship(src, dst, phase, landing, "col", stem + core)

    near = lax.div(c, depth)
    strip = jnp.where(c < 2, 0, jnp.where(c >= nc - 2, 1, 2 + near))
    order = [(1 - lax.div(near, 2)) * 2 + (1 - lax.rem(near, 2)), (1 - lax.div(near, 2)) * 2 + lax.rem(near, 2),
             lax.div(near, 2) * 2 + (1 - lax.rem(near, 2)), near]

    def arrived(phase, part):
        pltpu.make_async_copy(part, part, recv.at[phase]).wait()

    def left(phase, part):
        pltpu.make_async_copy(part, part, send.at[phase]).wait()

    def send_wave(v, far):
        if v == 0:
            to_col(1, 1, lambda peer: wa.at[:, sixteen(peer), :], wrow_a.at[c], far)
        else:
            to_col(2, 2, lambda peer: wbt.at[:, sixteen(peer), :], wrow_b.at[nc - 1 - c], far)

    for far in (True, False):
        to_col(0, 0, lambda peer: vol.at[:, sixteen(peer), :], rows0.at[c], far)
    for copy in loads[1:]:
        copy.wait()
    rows0[c] = vol[:, sixteen(c), :]
    wrow_a[c] = wa[:, sixteen(c), :]

    eye = one_hot(iota((BLOCK, BLOCK), 0) == iota((BLOCK, BLOCK), 1))
    anti = one_hot(iota((BLOCK, BLOCK), 0) == BLOCK - 1 - iota((BLOCK, BLOCK), 1))

    lane = iota((LINES, 128), 1)

    def table(offset):
        row = iota((256, WIN), 0) - offset
        row = jnp.where(iota((256, WIN), 0) < offset - 64, row + 256, row)
        return dot(one_hot(row == iota((256, WIN), 1)), fwd[...]).astype(BF)

    def merged(ref, start, count, offset):
        outer = jnp.where(
            iota((1, 1, LINES, 128), 3) < offset - 64, ref[pl.ds(start + 2, count)], ref[pl.ds(start, count)]
        )
        middle = ref[pl.ds(start + 1, count)]
        return jnp.concatenate([t.reshape(count * 2 * LINES, 128) for t in (outer, middle)], 1)

    def prepare(index, shifts, fractions, start, base, width):
        mine = iota((LINES, width), 1) == start + iota((LINES, width), 0)
        f = jnp.sum(jnp.where(mine, fractions, 0.0), axis=1, keepdims=True)
        k = jnp.sum(jnp.where(mine, shifts.astype(F32), 0.0), axis=1, keepdims=True)
        phase = (2.0 * np.pi / WIN) * f * lane.astype(F32)
        ramps[index, 0] = jnp.cos(phase)
        ramps[index, 1] = jnp.sin(phase)
        ramps[index, 2] = jnp.broadcast_to(k - base.astype(F32), (LINES, 128))
        offset = (-MARGIN - base) & 127
        tabs[index] = table(offset)

    def row_base(v, p):
        return jnp.minimum(srs[v, p, c * LINES], srs[v, p, c * LINES + LINES - 1])

    def col_base(v):
        return jnp.minimum(scs[v, r * LINES], scs[v, r * LINES + LINES - 1])

    for v in range(2):
        for p in range(2):
            prepare(3 * v + 2 * p, sr[v, pl.ds(p, 1), :], fr[v, pl.ds(p, 1), :], c * LINES, row_base(v, p), tile_rows)
        prepare(3 * v + 1, sc[pl.ds(v, 1), :], fc[pl.ds(v, 1), :], r * LINES, col_base(v), BLOCK)
    tabs[6] = table(jnp.int32(96))

    for part in range(2):
        flipped = dot(anti, wb[part]).astype(BF)
        for n in range(quarters):
            wbt[part, n * BLOCK : (n + 1) * BLOCK, :] = dot_nt(eye, flipped[:, n * BLOCK : (n + 1) * BLOCK]).astype(BF)

    zone[...] = jnp.zeros(zone.shape, BF)
    for v in range(2):
        ub[v, 0] = jnp.zeros((2, LINES, 128), BF)
        ub[v, col_tiles + 1] = jnp.zeros((2, LINES, 128), BF)

    pad = 14

    def shear(index, base, bits, src, count, dst, side, after):
        shift = ramps[index, 2].astype(jnp.int32)
        a = src[...].astype(F32)
        zero = jnp.zeros((1, 2, LINES, 128), F32)
        a = jnp.concatenate([a, zero], 0)
        for bit in range(bits):
            step = 2**bit
            turned = pltpu.roll(a, step, 3)
            before = jnp.concatenate([zero, turned[:-1]], 0)
            moved = jnp.where(lane >= step, turned, before)
            a = jnp.where((shift & step) != 0, moved, a)
        zone[pad : pad + count + 1] = a.astype(BF)
        first = lax.shift_right_arithmetic(-MARGIN - base, 7) + pad
        offset = (-MARGIN - base) & 127
        cosine = ramps[index, 0]
        sine = ramps[index, 1]
        group = count // 2
        for far in (True, False):
            m = (1 - side if far else side) * group
            spectrum = dot(merged(zone, first + m, group, offset), tabs[index])
            even = spectrum[:, :128].reshape(group * 2, LINES, 128)
            odd = spectrum[:, 128:].reshape(group * 2, LINES, 128)
            y = jnp.concatenate([even * cosine - odd * sine, odd * cosine + even * sine], 2)
            line = dot(y.reshape(group * 2 * LINES, 256).astype(BF), inv[...])
            dst[pl.ds(m, group)] = line.reshape(group, 2, LINES, 128).astype(BF)
            after(far)

    send_wave(0, True)
    send_wave(1, True)
    for v in range(2):
        if v == 0:
            arrived(0, rows0.at[pl.ds(0, nc - 1)])

        def after(far, v=v):
            to_col(3 + v, 17 + 4 * v + near, lambda peer: o1.at[v, peer], tile1.at[v, :, sixteen(c), :], far)

        shear(3 * v, row_base(v, 0), 3, rows0, col_tiles, o1.at[v], side_c, after)
        tile1[v, :, sixteen(c), :] = o1[v, c]

    def collected(landing, part, number):
        whole = part.at[:, pl.ds(0, number * LINES), :]
        pltpu.make_async_copy(whole, whole, recv.at[landing]).wait()

    def landed(landing, part, own):
        collected(landing, part, depth - 1 if own else depth)

    def rows_to_columns(v, which=(0, 1, 2, 3)):
        for i in which:
            k = order[i]
            spot = pl.ds(pl.multiple_of(k * BLOCK, BLOCK), BLOCK)
            landed(17 + 4 * v + k, tile1.at[v], i == 3)
            for part in range(2):
                turn1[v, k, part] = dot_nt(eye, tile1[v, part, spot, :]).astype(BF)
            for far in (False, True):
                to_row(
                    5 + v, 5 + v, lambda peer: turn1.at[v, k, :, sixteen(peer), :], cols.at[v, r * quarters + k], far
                )
            cols[v, r * quarters + k] = turn1[v, k, :, sixteen(r), :]

    def shear_columns(v):
        arrived(5 + v, cols.at[v, pl.ds(0, row_tiles - quarters)])

        shear(3 * v + 1, col_base(v), 4, cols.at[v], row_tiles, o2.at[v], side_r, lambda far: None)
        for k in order:
            for far in (False, True):
                to_row(
                    7 + v, 25 + 4 * v + k, lambda peer: o2.at[v, peer * quarters + k],
                    turn2.at[v, k, :, sixteen(r), :], far,
                )
        turn2[v, :, :, sixteen(r), :] = o2[v, pl.ds(r * quarters, quarters)]

    def columns_to_rows(v, which=(0, 1, 2, 3)):
        for i in which:
            k = order[i]
            spot = pl.ds(pl.multiple_of(k * BLOCK, BLOCK), BLOCK)
            arrived(25 + 4 * v + k, turn2.at[v, 0, :, pl.ds(0, BLOCK - LINES), :])
            for part in range(2):
                tile2[v, part, spot, :] = dot_nt(eye, turn2[v, k, part]).astype(BF)
            to_quarter(9 + v, 9 + v, lambda peer: tile2.at[v, :, sixteen(peer), :], rows2.at[v, c], k, (2, 1, 3, 0) if i % 2 else (0, 1, 3, 2), i == 3)
        if which[-1] == 3:
            rows2[v, c] = tile2[v, :, sixteen(c), :]

    wrow_b[nc - 1 - c] = wbt[:, sixteen(c), :]
    send_wave(0, False)
    send_wave(1, False)
    rows_to_columns(0)
    rows_to_columns(1)
    shear_columns(0)
    shear_columns(1)
    columns_to_rows(0)
    columns_to_rows(1)

    for v in range(2):
        wave = (wrow_a, wrow_b)[v]
        arrived(9 + v, rows2.at[v, pl.ds(0, nc - 1)])
        shear(3 * v + 2, row_base(v, 1), 3, rows2.at[v], col_tiles, rot, side_c, lambda far: None)
        arrived(1 + v, wave.at[pl.ds(0, nc - 1)])
        group = 8

        def through(g, _, v=v, wave=wave):
            m = g * group
            block = rot[pl.ds(m, group)].astype(F32)
            w = wave[pl.ds(m, group)].astype(F32)
            amplitude = jnp.exp(-ABSORB * block[:, 1])
            cosine, sine = cos_sin(block[:, 0])
            real = amplitude * cosine
            imaginary = amplitude * sine
            ub[v, pl.ds(1 + m, group), 0] = (w[:, 0] * real - w[:, 1] * imaginary).astype(BF)
            ub[v, pl.ds(1 + m, group), 1] = (w[:, 0] * imaginary + w[:, 1] * real).astype(BF)
            return 0

        lax.fori_loop(0, col_tiles // group, through, 0)
        phase = travel_phase(trav[v], iota((1, 256), 1) & 127)
        factor_real = jnp.cos(phase)
        factor_imaginary = jnp.sin(phase)
        span = col_tiles // 2
        spot = pl.ds(pl.multiple_of(MARGIN + c * LINES, LINES), LINES)
        for far in (True, False):
            m = (side_c if far == (v == 1) else 1 - side_c) * span
            spectrum = dot(merged(ub.at[v], m, span, 96), tabs[6]).reshape(span, 2, LINES, 256)
            a, b = spectrum[:, 0], spectrum[:, 1]
            y = jnp.stack([factor_real * a - factor_imaginary * b, factor_real * b + factor_imaginary * a], 1)
            line = dot(y.reshape(span * 2 * LINES, 256).astype(BF), inv[...])
            half[v, pl.ds(m, span)] = line.reshape(span, 2, LINES, 128).astype(BF)
            if v == 0:
                to_col(11, 33 + strip, lambda peer: half.at[0, peer], ext.at[0, :, spot, :], far)
            else:
                to_col(12, 39 + strip, lambda peer: half.at[1, nc - 1 - peer], ext.at[1, :, spot, :], far)
        ext[v, :, spot, :] = half[v, c if v == 0 else nc - 1 - c]

    top = pl.ds(0, MARGIN)
    bottom = pl.ds(MARGIN + tile_rows, MARGIN)
    head = pl.ds(MARGIN, MARGIN)
    tail = pl.ds(tile_rows, MARGIN)

    def down(v):
        return pltpu.make_async_remote_copy(
            src_ref=ext.at[v, :, tail, :], dst_ref=ext.at[v, :, top, :], send_sem=send.at[13 + v],
            recv_sem=recv.at[13 + v], device_id={"row": lax.rem(r + 1, nr)}, device_id_type=MESH,
        )

    def up(v):
        return pltpu.make_async_remote_copy(
            src_ref=ext.at[v, :, head, :], dst_ref=ext.at[v, :, bottom, :], send_sem=send.at[15 + v],
            recv_sem=recv.at[15 + v], device_id={"row": lax.rem(r + nr - 1, nr)}, device_id_type=MESH,
        )

    phase = travel_phase(trav[0], iota((256, 128), 0) & 127)
    down_real, down_imaginary = jnp.cos(phase), jnp.sin(phase)
    phase = travel_phase(trav[1], iota((1, 256), 1) & 127)
    along_real, along_imaginary = jnp.cos(phase), jnp.sin(phase)

    def finish(v, blocks):
        count = len(blocks)
        rows = [slice(n * BLOCK, n * BLOCK + WIN) for n in blocks]
        spots = [slice(n * BLOCK, (n + 1) * BLOCK) for n in blocks]
        if v == 0:
            window = jnp.concatenate([ext[0, part, at, :] for part in range(2) for at in rows], 1)
            spectrum = dot(fwdt[...], window)
            a, b = spectrum[:, : count * 128], spectrum[:, count * 128 :]
            real, imaginary = (jnp.concatenate([x] * count, 1) for x in (down_real, down_imaginary))
            y = jnp.concatenate([real * a - imaginary * b, real * b + imaginary * a], 1)
            line = dot(invt[...], y.astype(BF)).astype(BF)
            for part in range(2):
                for i, at in enumerate(spots):
                    out_a[part, at, :] = line[:, (part * count + i) * 128 : (part * count + i + 1) * 128]
        else:
            window = jnp.concatenate(
                [dot_nt(anti, ext[1, part, at, :]).astype(BF) for part in range(2) for at in rows], 0
            )
            spectrum = dot(window, fwd[...])
            a, b = spectrum[: count * BLOCK], spectrum[count * BLOCK :]
            y = jnp.concatenate([along_real * a - along_imaginary * b, along_real * b + along_imaginary * a], 0)
            line = dot(y.astype(BF), inv[...]).astype(BF)
            for part in range(2):
                for i, at in enumerate(spots):
                    out_b[part, :, at] = line[(part * count + i) * BLOCK : (part * count + i + 1) * BLOCK]

    counts = [2, 2, depth - 2] + [depth] * (quarters - 2) + [depth - 2]
    for v in range(2):
        for k in range(quarters + 2):

            @pl.when(strip == k)
            def _(v=v, k=k):
                collected(33 + 6 * v + k, ext.at[v], counts[k] - 1)

            @pl.when(strip != k)
            def _(v=v, k=k):
                collected(33 + 6 * v + k, ext.at[v], counts[k])

            if k == 0:

                @pl.when(r > 0)
                def _(v=v):
                    up(v).start()

                @pl.when(r == 0)
                def _(v=v):
                    ext[v, :, top, :] = jnp.zeros((2, MARGIN, 128), BF)

            if k == 1:

                @pl.when(r < nr - 1)
                def _(v=v):
                    down(v).start()

                @pl.when(r == nr - 1)
                def _(v=v):
                    ext[v, :, bottom, :] = jnp.zeros((2, MARGIN, 128), BF)

        finish(v, tuple(range(1, quarters - 1)))

        @pl.when(r > 0)
        def _(v=v):
            down(v).wait_recv()

        @pl.when(r < nr - 1)
        def _(v=v):
            up(v).wait_recv()

        finish(v, (0, quarters - 1))

    left(0, vol.at[:, pl.ds(0, tile_rows - LINES), :])
    left(1, wa.at[:, pl.ds(0, tile_rows - LINES), :])
    left(2, wbt.at[:, pl.ds(0, tile_rows - LINES), :])
    for v in range(2):
        left(3 + v, o1.at[v, pl.ds(0, nc - 1)])
        left(5 + v, turn1.at[v, :, :, pl.ds(0, BLOCK - LINES), :])
        left(7 + v, o2.at[v, pl.ds(0, row_tiles - quarters)])
        left(9 + v, tile2.at[v, :, pl.ds(0, tile_rows - LINES), :])
        left(11 + v, half.at[v, pl.ds(0, nc - 1)])

        @pl.when(r < nr - 1)
        def _(v=v):
            down(v).wait_send()

        @pl.when(r > 0)
        def _(v=v):
            up(v).wait_send()


def on_device(nr, nc, vol, wa, wb, sr, fr, sc, fc, trav):
    forward, inverse = real_tables()
    tile_rows = nc * LINES
    quarters = tile_rows // BLOCK
    col_tiles, row_tiles = nc, nr * quarters
    anywhere = pl.BlockSpec(memory_space=pl.ANY)
    lines = (2, LINES, 128)
    scratch = [
        pltpu.VMEM((2, tile_rows, 128), BF),
        pltpu.VMEM((2, tile_rows, 128), BF),
        pltpu.VMEM((2, BLOCK, tile_rows), BF),
        pltpu.SMEM(sr.shape, jnp.int32),
        pltpu.SMEM(sc.shape, jnp.int32),
        pltpu.SMEM(trav.shape, F32),
        pltpu.VMEM(sr.shape, jnp.int32),
        pltpu.VMEM(fr.shape, F32),
        pltpu.VMEM(sc.shape, jnp.int32),
        pltpu.VMEM(fc.shape, F32),
        pltpu.VMEM((WIN, 256), BF),
        pltpu.VMEM((256, BLOCK), BF),
        pltpu.VMEM((256, WIN), BF),
        pltpu.VMEM((BLOCK, 256), BF),
        pltpu.SemaphoreType.DMA((14,)),
        pltpu.VMEM((2, tile_rows, 128), BF),
        pltpu.VMEM((col_tiles, *lines), BF),
        pltpu.VMEM((col_tiles, *lines), BF),
        pltpu.VMEM((col_tiles, *lines), BF),
        pltpu.VMEM((64, *lines), BF),
        pltpu.VMEM((2, col_tiles, *lines), BF),
        pltpu.VMEM((2, 2, tile_rows, 128), BF),
        pltpu.VMEM((2, quarters, 2, BLOCK, 128), BF),
        pltpu.VMEM((2, row_tiles, *lines), BF),
        pltpu.VMEM((2, row_tiles, *lines), BF),
        pltpu.VMEM((2, quarters, 2, BLOCK, 128), BF),
        pltpu.VMEM((2, 2, tile_rows, 128), BF),
        pltpu.VMEM((2, col_tiles, *lines), BF),
        pltpu.VMEM((col_tiles, *lines), BF),
        pltpu.VMEM((2, col_tiles + 2, *lines), BF),
        pltpu.VMEM((2, col_tiles, *lines), BF),
        pltpu.VMEM((2, 2, tile_rows + 2 * MARGIN, 128), BF),
        pltpu.VMEM((6, 3, LINES, 128), F32),
        pltpu.VMEM((7, 256, 256), BF),
        pltpu.SemaphoreType.DMA((17,)),
        pltpu.SemaphoreType.DMA((45,)),
    ]
    result = pl.pallas_call(
        functools.partial(kernel, nr, nc),
        out_shape=(
            pltpu.VMEM((2, tile_rows, 128), BF),
            pltpu.VMEM((2, 128, tile_rows), BF),
        ),
        in_specs=[pl.BlockSpec(memory_space=pltpu.HBM)] * 12,
        out_specs=(pl.BlockSpec(memory_space=pltpu.VMEM),) * 2,
        scratch_shapes=scratch,
        compiler_params=pltpu.CompilerParams(
            collective_id=0, has_side_effects=True, vmem_limit_bytes=65994752
        ),
        name="rotate_travel",
    )(
        vol, wa, wb, sr, fr, sc, fc, trav,
        jnp.asarray(forward, BF), jnp.asarray(inverse, BF),
        jnp.asarray(forward.T, BF), jnp.asarray(inverse.T, BF),
    )
    return pl.pallas_call(
        hand_over,
        out_shape=tuple(jax.ShapeDtypeStruct(x.shape, x.dtype) for x in result),
        in_specs=[anywhere] * 2,
        out_specs=(anywhere, anywhere),
        scratch_shapes=[pltpu.SemaphoreType.DMA((2,))],
        compiler_params=pltpu.CompilerParams(vmem_limit_bytes=2 * 2**20),
        name="hand_over",
    )(*result)


def hand_over(a, b, out_a, out_b, sem):
    given = [pltpu.make_async_copy(a, out_a, sem.at[0]), pltpu.make_async_copy(b, out_b, sem.at[1])]
    for copy in given:
        copy.start()
    for copy in given:
        copy.wait()


def solution(mesh):
    nr, nc = mesh.shape["row"], mesh.shape["col"]
    return jax.shard_map(
        functools.partial(on_device, nr, nc),
        mesh=mesh,
        in_specs=(
            P(None, "row", "col"),
            P(None, "row", "col"),
            P(None, "col", "row"),
            P(None, None, "row"),
            P(None, None, "row"),
            P(None, "col"),
            P(None, "col"),
            P(),
        ),
        out_specs=(P(None, "row", "col"), P(None, "col", "row")),
        check_vma=False,
    )
```
